32 devices in a mesh: shock: 16 (over z, x, core), trans: 2 (over y).
Axes of the slice: x: 2, y: 2, z: 4, core: 2. Of those that a mesh axis runs over, the one named last changes fastest.
Arguments:
- displacement: float32 [3, 8192], P(None, ('shock', 'trans')), may hold values from -0.32 to 0.32
- velocity: float32 [3, 8192], P(None, ('shock', 'trans')), may hold values from -4 to 4
- force_before: float32 [3, 8192], P(None, ('shock', 'trans')), may hold values from -4 to 4
- beta: float32 [50], replicated, may hold values from -0.875 to 0.875
- alpha: float32 [50, 50], replicated, may hold values from -0.125 to 0.125
- live_count: int32 [32], P(('shock', 'trans')), may hold values from 128 to 256, as said below
- trans_send: int32 [2, 1024], P(None, ('shock', 'trans')), may hold values from 0 to 127, as said below
- shock_send: int32 [2, 4096], P(None, ('shock', 'trans')), may hold values from 0 to 319, as said below
- neighbour_block: int32 [26, 8192], P(None, ('shock', 'trans')), may hold values from -1 to 4, as said below
- neighbour_lane: int32 [26, 8192], P(None, ('shock', 'trans')), may hold values from 0 to 127, as said below
- leaving_slots: int32 [512], P(('shock', 'trans')), may hold values from 0 to 127, as said below
- leaving_count: int32 [32], P(('shock', 'trans')), may hold values from 8 to 16, as said below
Outputs:
- displacement_next: float32 [3, 8192], P(None, ('shock', 'trans'))
- velocity_next: float32 [3, 8192], P(None, ('shock', 'trans'))
- force_next: float32 [3, 8192], P(None, ('shock', 'trans'))
- atom_energy: float32 [8192], P(('shock', 'trans'))
- arrivals: float32 [3, 3, 512], P(None, None, ('shock', 'trans'))
The draws below stay inside these ranges and needn't reach their ends.
Inputs may be any that keep to these rules, and one draw needn't show every extreme that they name: A store's live atoms are its slots 0 to live_count - 1; stores at the lowest shock indices, behind the front, are full, and some store holds 256. `trans_send`: entries are live atoms of the sending store. `shock_send`: entries are live atoms or transverse ghost columns of the sending store's first section. `neighbour_block`: -1 marks an absent neighbour; slots at or above live_count have none; otherwise the column names a live own atom or a ghost column, never a ghost block beyond an open end of the shock axis. `neighbour_lane`: read together with neighbour_block. `leaving_slots`: distinct live atoms of the store. `leaving_count`: some store uses all 16 entries.
All inputs are finite; a program needn't handle non-finite values.
Results may differ from the reference program's by a relative error of at most 0.0003.
Values sent between devices are 32-bit elements; how exact they have to be, the bound alone decides.
No kernel may reach another device: no remote copies, remote signals or barrier semaphores. Data moves between devices by JAX's collectives and lax.ppermute only.
A program may use at most 64 MiB of HBM per device.

```python
import math
import jax
import jax.numpy as jnp
import numpy as np
from jax import lax

ATOM_SLOTS = 256
NEIGHBOURS = 26
DESCRIPTORS = 50
TRANS_GHOSTS = 32
SHOCK_GHOSTS = 128
LEAVE_SLOTS = 16
ATOMS_ALL = 8192
N_SHOCK = 16
N_TRANS = 2
DEVICES = 32


def store_counts(key):
    front_index = jax.random.randint(jax.random.fold_in(key, 101), (), N_SHOCK // 4, N_SHOCK - N_SHOCK // 4 + 1)
    shock_index = jnp.arange(DEVICES, dtype=jnp.int32) // N_TRANS
    uncompressed = jax.random.randint(jax.random.fold_in(key, 102), (DEVICES,), ATOM_SLOTS // 2, ATOM_SLOTS // 2 + ATOM_SLOTS // 8 + 1)
    return jnp.where(shock_index < front_index, ATOM_SLOTS, uncompressed).astype(jnp.int32)


def neighbour_index(key):
    counts = store_counts(key)
    compressed = counts == ATOM_SLOTS
    full_shape = (NEIGHBOURS, DEVICES, ATOM_SLOTS)
    slot_index = jnp.arange(ATOM_SLOTS, dtype=jnp.int32)[None, None, :]
    entry_index = jnp.arange(NEIGHBOURS, dtype=jnp.int32)[:, None, None]
    shock_index = (jnp.arange(DEVICES, dtype=jnp.int32) // N_TRANS)[None, :, None]
    additional = jax.random.randint(jax.random.fold_in(key, 201), full_shape, 0, 4) == 0
    occupied = (slot_index < counts[None, :, None]) & (compressed[None, :, None] | (entry_index < 14) | additional)
    category = jax.random.randint(jax.random.fold_in(key, 202), full_shape, 0, 10)
    own_pick = jax.random.randint(jax.random.fold_in(key, 203), full_shape, 0, counts[None, :, None])
    trans_pick = jax.random.randint(jax.random.fold_in(key, 204), full_shape, 0, TRANS_GHOSTS)
    shock_pick = jax.random.randint(jax.random.fold_in(key, 205), full_shape, 0, SHOCK_GHOSTS)
    first_width = ATOM_SLOTS + 2 * TRANS_GHOSTS
    chosen = jnp.where(category == 0, ATOM_SLOTS + trans_pick, own_pick)
    chosen = jnp.where(category == 1, ATOM_SLOTS + TRANS_GHOSTS + trans_pick, chosen)
    chosen = jnp.where((category == 2) & (shock_index > 0), first_width + shock_pick, chosen)
    chosen = jnp.where((category == 3) & (shock_index < N_SHOCK - 1), first_width + SHOCK_GHOSTS + shock_pick, chosen)
    chosen = jnp.where(occupied, chosen, -1).astype(jnp.int32)
    return chosen.reshape(NEIGHBOURS, DEVICES * ATOM_SLOTS)


def draw_live_count(key, part):
    return store_counts(key)


def draw_trans_send(key, part):
    picks = jax.random.randint(jax.random.fold_in(key, 301), (2, DEVICES, TRANS_GHOSTS), 0, ATOM_SLOTS // 2)
    return picks.reshape(2, DEVICES * TRANS_GHOSTS).astype(jnp.int32)


def draw_shock_send(key, part):
    full_shape = (2, DEVICES, SHOCK_GHOSTS)
    category = jax.random.randint(jax.random.fold_in(key, 401), full_shape, 0, 8)
    own_pick = jax.random.randint(jax.random.fold_in(key, 402), full_shape, 0, ATOM_SLOTS // 2)
    ghost_pick = ATOM_SLOTS + jax.random.randint(jax.random.fold_in(key, 403), full_shape, 0, 2 * TRANS_GHOSTS)
    return jnp.where(category == 0, ghost_pick, own_pick).reshape(2, DEVICES * SHOCK_GHOSTS).astype(jnp.int32)


def draw_neighbour_block(key, part):
    return neighbour_index(key) // 128


def draw_neighbour_lane(key, part):
    return neighbour_index(key) % 128


def draw_leaving_slots(key, part):
    stride = ATOM_SLOTS // 2 // LEAVE_SLOTS
    starting = jnp.arange(LEAVE_SLOTS, dtype=jnp.int32) * stride
    jitter = jax.random.randint(jax.random.fold_in(key, 501), (DEVICES, LEAVE_SLOTS), 0, stride)
    return (starting[None, :] + jitter).reshape(DEVICES * LEAVE_SLOTS).astype(jnp.int32)


def draw_leaving_count(key, part):
    counts = jax.random.randint(jax.random.fold_in(key, 601), (DEVICES,), LEAVE_SLOTS // 2, LEAVE_SLOTS + 1)
    fullest = jax.random.randint(jax.random.fold_in(key, 602), (), 0, DEVICES)
    return jnp.where(jnp.arange(DEVICES) == fullest, LEAVE_SLOTS, counts).astype(jnp.int32)


def block_levels(stream_key, extent, cuts, least, top_value):
    def one(axis_at, shards_of):
        heights = jax.random.uniform(jax.random.fold_in(jax.random.fold_in(stream_key, 6), axis_at), (shards_of,), jnp.float32, least / len(cuts), top_value / len(cuts))
        return jnp.repeat(jnp.exp(heights), extent[axis_at] // shards_of).reshape((-1,) + (1,) * (len(extent) - axis_at - 1))

    level = one(*cuts[0])
    for cut in cuts[1:]:
        level = level * one(*cut)
    return level


def normal_values(key, dims, spread, reach, pieces=(), kind=jnp.bfloat16):
    drawn = jax.random.normal(key, dims, jnp.float32) * spread
    if len(pieces) > 0:
        drawn = block_levels(key, dims, pieces, -0.22, 0.18) * drawn
    return jnp.clip(drawn, min=-reach, max=reach).astype(kind)


def setup_inputs(seed: int = 0) -> dict:
    key_of = jax.random.split(jax.random.key(seed), 13)
    displacement = normal_values(key_of[0], (3, ATOMS_ALL), 0.08, 0.32, ((1, 32),), jnp.float32)
    velocity = normal_values(key_of[1], (3, ATOMS_ALL), 1.0, 4.0, ((1, 32),), jnp.float32)
    force_before = normal_values(key_of[2], (3, ATOMS_ALL), 1.0, 4.0, ((1, 32),), jnp.float32)
    beta = normal_values(key_of[3], (DESCRIPTORS,), DESCRIPTORS ** -0.5, 0.875, (), jnp.float32)
    alpha = normal_values(key_of[4], (DESCRIPTORS, DESCRIPTORS), (DESCRIPTORS * DESCRIPTORS) ** -0.5, 0.125, (), jnp.float32)
    live_count = draw_live_count(jax.random.fold_in(key_of[12], 71), 0)
    trans_send = draw_trans_send(jax.random.fold_in(key_of[12], 71), 0)
    shock_send = draw_shock_send(jax.random.fold_in(key_of[12], 71), 0)
    neighbour_block = draw_neighbour_block(jax.random.fold_in(key_of[12], 71), 0)
    neighbour_lane = draw_neighbour_lane(jax.random.fold_in(key_of[12], 71), 0)
    leaving_slots = draw_leaving_slots(jax.random.fold_in(key_of[12], 71), 0)
    leaving_count = draw_leaving_count(jax.random.fold_in(key_of[12], 71), 0)
    return {"displacement": displacement, "velocity": velocity, "force_before": force_before, "beta": beta, "alpha": alpha, "live_count": live_count, "trans_send": trans_send, "shock_send": shock_send, "neighbour_block": neighbour_block, "neighbour_lane": neighbour_lane, "leaving_slots": leaving_slots, "leaving_count": leaving_count}


kick_factor = 0.5
drift_step = 0.02
cutoff_radius = 4.2
radial_width = 0.35
radial_centers = (1.4, 1.9, 2.4, 2.9)
moment_scale = 0.25
pair_list = ((0, 0), (0, 1), (0, 2), (0, 3), (1, 1), (1, 2), (1, 3), (2, 2), (2, 3), (3, 3))
highest = lax.Precision.HIGHEST

def lattice_table():
    entries = []
    for number in range(8):
        entries.append([1.0 - 2.0 * (number >> 2 & 1), 1.0 - 2.0 * (number >> 1 & 1), 1.0 - 2.0 * (number & 1)])
    for axis_pick in range(3):
        for signed in (2.0, -2.0):
            vector = [0.0, 0.0, 0.0]
            vector[axis_pick] = signed
            entries.append(vector)
    for zero_pick in (2, 1, 0):
        others = [axis_pick for axis_pick in range(3) if axis_pick != zero_pick]
        for leading in (2.0, -2.0):
            for trailing in (2.0, -2.0):
                vector = [0.0, 0.0, 0.0]
                vector[others[0]] = leading
                vector[others[1]] = trailing
                entries.append(vector)
    return np.array(entries, dtype=np.float32).T

def exponent_table():
    triples = []
    for degree in range(5):
        for first_power in range(degree, -1, -1):
            for second_power in range(degree - first_power, -1, -1):
                triples.append((degree, first_power, second_power, degree - first_power - second_power))
    return triples

def contraction_weights():
    triples = exponent_table()
    matrix = np.zeros((5, len(triples)), dtype=np.float32)
    for column, (degree, first_power, second_power, third_power) in enumerate(triples):
        matrix[degree, column] = math.factorial(degree) / (math.factorial(first_power) * math.factorial(second_power) * math.factorial(third_power))
    return matrix

def block_energy(vectors, present, beta, alpha):
    distance = jnp.sqrt(lax.optimization_barrier(jnp.sum(vectors * vectors, axis=0)))
    direction = vectors / distance[None]
    smooth = 0.5 * (jnp.cos(jnp.pi * distance / cutoff_radius) + 1.0) * present
    radial = jnp.stack([smooth * jnp.exp(-jnp.square((distance - center) / radial_width)) for center in radial_centers])
    powers_first = [jnp.ones_like(distance)]
    powers_second = [jnp.ones_like(distance)]
    powers_third = [jnp.ones_like(distance)]
    for degree in range(4):
        powers_first.append(powers_first[-1] * direction[0])
        powers_second.append(powers_second[-1] * direction[1])
        powers_third.append(powers_third[-1] * direction[2])
    monomials = jnp.stack([powers_first[first_power] * powers_second[second_power] * powers_third[third_power] for degree, first_power, second_power, third_power in exponent_table()])
    moments = moment_scale * jnp.einsum('nkb,mkb->nmb', radial, monomials, precision=highest)
    products = jnp.stack([moments[first_index] * moments[second_index] for first_index, second_index in pair_list])
    weights = jnp.asarray(contraction_weights())
    descriptor = jnp.einsum('lm,pmb->plb', weights, products, precision=highest)
    descriptor = descriptor.reshape(len(pair_list) * 5, descriptor.shape[2])
    linear = jnp.dot(beta, descriptor, precision=highest)
    quadratic = lax.optimization_barrier(jnp.sum(descriptor * jnp.dot(alpha, descriptor, precision=highest), axis=0))
    return linear + 0.5 * quadratic

def store_terms(extended, own_rows, neighbour_block, neighbour_lane, beta, alpha):
    slot_count = own_rows.shape[1]
    block_rows = min(slot_count, 2048)
    groups = slot_count // block_rows
    offsets = jnp.asarray(lattice_table())
    present = neighbour_block >= 0
    clamped = jnp.where(present, neighbour_block * 128 + neighbour_lane, 0).astype(jnp.int32)
    weight_live = present.astype(extended.dtype)

    def one_group(inputs):
        clamped_rows, live_rows, own_group = inputs
        vectors = offsets[:, :, None] + extended[:, clamped_rows] - own_group[:, None, :]
        energies, pullback = jax.vjp(lambda moved: block_energy(moved, live_rows, beta, alpha), vectors)
        pair_grad, = pullback(jnp.ones_like(energies))
        return (energies, pair_grad)

    def grouped(array):
        return jnp.moveaxis(array.reshape(array.shape[:-1] + (groups, block_rows)), -2, 0)
    energies, pair_grad = lax.map(one_group, (grouped(clamped), grouped(weight_live), grouped(own_rows)))
    energies = energies.reshape(slot_count)
    pair_grad = jnp.moveaxis(pair_grad, 0, -2).reshape(3, clamped.shape[0], slot_count)
    total = jnp.zeros((3, extended.shape[1]), extended.dtype)
    total = total.at[:, clamped.reshape(-1)].add(pair_grad.reshape(3, -1))
    total = total.at[:, :slot_count].add(-lax.optimization_barrier(jnp.sum(pair_grad, axis=1)))
    return (energies, total)

def pick_columns(stores, lists):
    return jax.vmap(lambda store_rows, index_rows: store_rows[:, index_rows], in_axes=(1, 1), out_axes=2)(stores, lists)

def add_columns(stores, lists, values):

    def one_store(store_rows, index_rows, value_rows):
        return store_rows.at[:, index_rows[0]].add(value_rows[:, 0]).at[:, index_rows[1]].add(value_rows[:, 1])
    return jax.vmap(one_store, in_axes=(1, 1, 2), out_axes=1)(stores, lists, values)

def reference(displacement, velocity, force_before, beta, alpha, live_count, trans_send, shock_send, neighbour_block, neighbour_lane, leaving_slots, leaving_count):
    half_velocity = velocity + kick_factor * force_before
    displaced = displacement + drift_step * half_velocity
    own_grid = displaced.reshape(3, DEVICES, ATOM_SLOTS)
    trans_lists = trans_send.reshape(2, DEVICES, TRANS_GHOSTS)
    shock_lists = shock_send.reshape(2, DEVICES, SHOCK_GHOSTS)
    first_width = ATOM_SLOTS + 2 * TRANS_GHOSTS
    sent = pick_columns(own_grid, trans_lists).reshape(3, 2, N_SHOCK, N_TRANS, TRANS_GHOSTS)
    from_lower = jnp.roll(sent[:, 1], 1, axis=2)
    from_upper = jnp.roll(sent[:, 0], -1, axis=2)
    first_section = jnp.concatenate([own_grid.reshape(3, N_SHOCK, N_TRANS, ATOM_SLOTS), from_lower, from_upper], axis=3)
    sent = pick_columns(first_section.reshape(3, DEVICES, first_width), shock_lists).reshape(3, 2, N_SHOCK, N_TRANS, SHOCK_GHOSTS)
    empty = jnp.zeros((3, 1, N_TRANS, SHOCK_GHOSTS), displaced.dtype)
    from_lower = jnp.concatenate([empty, sent[:, 1, :-1]], axis=1)
    from_upper = jnp.concatenate([sent[:, 0, 1:], empty], axis=1)
    extended = jnp.concatenate([first_section, from_lower, from_upper], axis=3).reshape(3, DEVICES, -1)
    block_grid = neighbour_block.reshape(NEIGHBOURS, DEVICES, ATOM_SLOTS)
    lane_grid = neighbour_lane.reshape(NEIGHBOURS, DEVICES, ATOM_SLOTS)

    def one_store(inputs):
        extended_rows, own_rows, block_rows, lane_rows = inputs
        return store_terms(extended_rows, own_rows, block_rows, lane_rows, beta, alpha)
    energies, gradients = lax.map(one_store, (jnp.moveaxis(extended, 1, 0), jnp.moveaxis(own_grid, 1, 0), jnp.moveaxis(block_grid, 1, 0), jnp.moveaxis(lane_grid, 1, 0)))
    gradient_grid = jnp.moveaxis(gradients, 0, 1).reshape(3, N_SHOCK, N_TRANS, -1)
    lower_ghosts = gradient_grid[..., first_width:first_width + SHOCK_GHOSTS]
    upper_ghosts = gradient_grid[..., first_width + SHOCK_GHOSTS:]
    back_lower = jnp.concatenate([empty, upper_ghosts[:, :-1]], axis=1)
    back_upper = jnp.concatenate([lower_ghosts[:, 1:], empty], axis=1)
    returned = jnp.stack([back_lower, back_upper], axis=1).reshape(3, 2, DEVICES, SHOCK_GHOSTS)
    first_grad = add_columns(gradient_grid[..., :first_width].reshape(3, DEVICES, first_width), shock_lists, returned)
    first_grid = first_grad.reshape(3, N_SHOCK, N_TRANS, first_width)
    lower_trans = first_grid[..., ATOM_SLOTS:ATOM_SLOTS + TRANS_GHOSTS]
    upper_trans = first_grid[..., ATOM_SLOTS + TRANS_GHOSTS:]
    back_lower = jnp.roll(upper_trans, 1, axis=2)
    back_upper = jnp.roll(lower_trans, -1, axis=2)
    returned = jnp.stack([back_lower, back_upper], axis=1).reshape(3, 2, DEVICES, TRANS_GHOSTS)
    own_grad = add_columns(first_grid[..., :ATOM_SLOTS].reshape(3, DEVICES, ATOM_SLOTS), trans_lists, returned)
    force_new = -own_grad
    velocity_new = half_velocity.reshape(3, DEVICES, ATOM_SLOTS) + kick_factor * force_new
    slot_index = jnp.arange(ATOM_SLOTS, dtype=jnp.int32)
    leave_index = jnp.arange(LEAVE_SLOTS, dtype=jnp.int32)
    leaving_grid = leaving_slots.reshape(DEVICES, LEAVE_SLOTS)
    sending = leave_index[None, :] < leaving_count[:, None]

    def departures(slot_rows, sending_rows):
        marked = jnp.zeros((ATOM_SLOTS + 1,), jnp.float32).at[jnp.where(sending_rows, slot_rows, ATOM_SLOTS).astype(jnp.int32)].set(1.0)
        return marked[:ATOM_SLOTS]
    departed = jax.vmap(departures)(leaving_grid, sending)
    retained = (slot_index[None, :] < live_count[:, None]).astype(jnp.float32) * (1.0 - departed)
    payload = jnp.stack([own_grid, velocity_new, force_new])
    chosen = jax.vmap(lambda quantities, index_rows: quantities[:, :, index_rows], in_axes=(2, 0), out_axes=2)(payload, leaving_grid)
    chosen = chosen * sending[None, None].astype(chosen.dtype)
    chosen = chosen.reshape(3, 3, N_SHOCK, N_TRANS, LEAVE_SLOTS)
    arrivals = jnp.concatenate([chosen[:, :, 1:], jnp.zeros_like(chosen[:, :, :1])], axis=2).reshape(3, 3, DEVICES * LEAVE_SLOTS)
    displacement_next = (own_grid * retained[None]).reshape(3, ATOMS_ALL)
    velocity_next = (velocity_new * retained[None]).reshape(3, ATOMS_ALL)
    force_next = (force_new * retained[None]).reshape(3, ATOMS_ALL)
    atom_energy = (energies * retained).reshape(ATOMS_ALL)
    return (displacement_next, velocity_next, force_next, atom_energy, arrivals)
```

```python
import math

import jax
import jax.numpy as jnp
import numpy as np
from jax import lax
from jax.experimental import pallas as pl
from jax.experimental.pallas import tpu as pltpu
from jax.sharding import PartitionSpec as P

kick_factor = 0.5
drift_step = 0.02
cutoff_radius = 4.2
radial_width = 0.35
radial_centers = (1.4, 1.9, 2.4, 2.9)
moment_scale = 0.25
pair_list = ((0, 0), (0, 1), (0, 2), (0, 3), (1, 1), (1, 2), (1, 3), (2, 2), (2, 3), (3, 3))
degrees = 5
lanes = 128
highest = lax.Precision.HIGHEST
f32 = jnp.float32
bf16 = jnp.bfloat16


def lattice_list():
    entries = []
    for number in range(8):
        entries.append(
            (1.0 - 2.0 * (number >> 2 & 1), 1.0 - 2.0 * (number >> 1 & 1), 1.0 - 2.0 * (number & 1))
        )
    for axis_pick in range(3):
        for signed in (2.0, -2.0):
            vector = [0.0, 0.0, 0.0]
            vector[axis_pick] = signed
            entries.append(tuple(vector))
    for zero_pick in (2, 1, 0):
        others = [axis_pick for axis_pick in range(3) if axis_pick != zero_pick]
        for leading in (2.0, -2.0):
            for trailing in (2.0, -2.0):
                vector = [0.0, 0.0, 0.0]
                vector[others[0]] = leading
                vector[others[1]] = trailing
                entries.append(tuple(vector))
    return entries


def exponent_list():
    return [
        (p, q, degree - p - q)
        for degree in range(degrees)
        for p in range(degree, -1, -1)
        for q in range(degree - p, -1, -1)
    ]


exponents = exponent_list()


def rows_of(value, count=8):
    return jnp.broadcast_to(value, (count,) + value.shape[1:])


def pick_lanes(table, index):
    return jnp.take_along_axis(table, index, axis=1, mode="promise_in_bounds")


def pick_columns(blocks, column):
    rows = blocks[0].shape[0]
    lane = rows_of(column & (lanes - 1), rows)
    block = rows_of(column >> 7, rows)
    out = jnp.zeros((rows, lanes), f32)
    for number, table in enumerate(blocks):
        out = jnp.where(block == number, pick_lanes(table, lane), out)
    return out


def pad_lanes(value, fill=0):
    rows, width = value.shape
    if width == lanes:
        return value
    return jnp.concatenate([value, jnp.full((rows, lanes - width), fill, value.dtype)], axis=1)


def pad_rows(value, count=8):
    rows = value.shape[0]
    return jnp.concatenate([value, jnp.zeros((count - rows,) + value.shape[1:], value.dtype)], axis=0)


def scatter_product(items, block_count):
    sub = lax.broadcasted_iota(jnp.int32, (8, lanes), 0)
    spot = lax.broadcasted_iota(jnp.int32, (lanes, lanes), 0)
    left = []
    right = []
    for value, lane, block in items:
        high = value.astype(bf16).astype(f32)
        part = jnp.where(sub < 3, high, value - high)
        block = rows_of(block)
        left.append(
            jnp.concatenate(
                [jnp.where(block == number, part, 0.0) for number in range(block_count)], axis=0
            ).astype(bf16)
        )
        right.append(
            jnp.where(spot == jnp.broadcast_to(lane, (lanes, lanes)), 1.0, 0.0).astype(bf16)
        )
    return lax.dot_general(
        jnp.concatenate(left, axis=1),
        jnp.concatenate(right, axis=1),
        (((1,), (1,)), ((), ())),
        preferred_element_type=f32,
    )


def twice(value):
    return jnp.concatenate([value, value, value[:2]], axis=0)


def summed(product, number):
    return product[8 * number : 8 * number + 3] + product[8 * number + 3 : 8 * number + 6]


def start_kernel(disp, vel, force, trans_send, displaced_out, trans_out):
    displaced = disp[...] + drift_step * (vel[...] + kick_factor * force[...])
    displaced_out[...] = displaced
    width = trans_send.shape[1]
    blocks = [
        pad_rows(displaced[:, lanes * b : lanes * (b + 1)]) for b in range(displaced.shape[1] // lanes)
    ]
    for way in range(2):
        column = pad_lanes(trans_send[way : way + 1, :])
        trans_out[way] = pick_columns(blocks, column)[:3, :width]


def shock_kernel(displaced, trans_in, shock_send, lower_out, upper_out, trans_block):
    width = trans_in.shape[2]
    trans_block[...] = jnp.zeros(trans_block.shape, f32)
    trans_block[:3, :width] = trans_in[1]
    trans_block[:3, width : 2 * width] = trans_in[0]
    blocks = [
        pad_rows(displaced[:, lanes * b : lanes * (b + 1)]) for b in range(displaced.shape[1] // lanes)
    ]
    blocks.append(trans_block[...])
    for way, out in enumerate((lower_out, upper_out)):
        out[...] = pick_columns(blocks, shock_send[way : way + 1, :])[:3]


def energy_kernel(
    displaced,
    trans_in,
    from_lower,
    from_upper,
    neighbour_block,
    neighbour_lane,
    beta,
    alpha,
    energy_out,
    own_out,
    trans_out,
    lower_out,
    upper_out,
    trans_block,
    spots,
    grads,
    packed,
    mono_store,
    grad_store,
):
    neighbours = neighbour_block.shape[0]
    slots = displaced.shape[1]
    width = trans_in.shape[2]
    halves = slots // lanes
    per_group = 8 // halves
    groups = -(-neighbours // per_group)
    own_blocks = halves
    block_count = own_blocks + 3
    sub = lax.broadcasted_iota(jnp.int32, (8, lanes), 0)
    half_of = sub % halves
    which = sub // halves

    def by_half(pieces):
        out = rows_of(pieces[0])
        for number in range(1, halves):
            out = jnp.where(half_of == number, rows_of(pieces[number]), out)
        return out

    def by_which(values):
        out = jnp.full((8, lanes), values[0], f32)
        for number in range(1, per_group):
            if any(v != values[0] for v in values):
                out = jnp.where(which == number, values[number], out)
        return out

    def over_group(value):
        shift = 4
        while shift >= halves:
            value = value + pltpu.roll(value, shift, 0)
            shift //= 2
        return value

    column = neighbour_block[...] * lanes + neighbour_lane[...]
    column = jnp.where(column >= slots + 2 * width, column + (lanes - 2 * width), column)
    column = jnp.where(neighbour_block[...] < 0, -1, column)
    spots[...] = jnp.full(spots.shape, -1, jnp.int32)
    for number in range(halves):
        spots[pl.ds(number, neighbours, stride=halves), :] = column[
            :, lanes * number : lanes * (number + 1)
        ]
    trans_block[...] = jnp.zeros(trans_block.shape, f32)
    trans_block[:3, :width] = trans_in[1]
    trans_block[:3, width : 2 * width] = trans_in[0]

    def table(axis):
        pieces = [displaced[axis : axis + 1, lanes * b : lanes * (b + 1)] for b in range(own_blocks)]
        pieces.append(trans_block[axis : axis + 1, :])
        pieces.append(from_lower[axis : axis + 1, :])
        pieces.append(from_upper[axis : axis + 1, :])
        return pieces

    tables = [table(axis) for axis in range(3)]
    own = [by_half(tables[axis][:own_blocks]) for axis in range(3)]
    spread = [[rows_of(piece) for piece in tables[axis]] for axis in range(3)]
    offsets = lattice_list()
    offsets = offsets + [offsets[0]] * (groups * per_group - neighbours)

    directions = []
    radials = []
    slopes = []
    inverses = []
    for group in range(groups):
        spot = spots[8 * group : 8 * group + 8, :]
        live = spot >= 0
        lane = jnp.where(live, spot & (lanes - 1), 0)
        block = jnp.where(live, spot >> 7, 0)
        vector = []
        for axis in range(3):
            picked = pick_lanes(spread[axis][0], lane)
            for number in range(1, block_count):
                picked = jnp.where(block == number, pick_lanes(spread[axis][number], lane), picked)
            offset = by_which([offsets[per_group * group + i][axis] for i in range(per_group)])
            vector.append(offset + picked - own[axis])
        square = vector[0] * vector[0] + vector[1] * vector[1] + vector[2] * vector[2]
        inverse = lax.rsqrt(square)
        distance = square * inverse
        directions.append([v * inverse for v in vector])
        inverses.append(inverse)
        angle = distance * (math.pi / cutoff_radius) - (math.pi / 2)
        squared = angle * angle
        sine = jnp.full_like(angle, -1.0 / math.factorial(15))
        for order in (13, 11, 9, 7, 5, 3, 1):
            sine = sine * squared + ((-1.0) ** ((order - 1) // 2)) / math.factorial(order)
        sine = sine * angle
        cosine = jnp.full_like(angle, 1.0 / math.factorial(16))
        for order in (14, 12, 10, 8, 6, 4, 2, 0):
            cosine = cosine * squared + ((-1.0) ** (order // 2)) / math.factorial(order)
        half = jnp.where(live, 0.5, 0.0)
        smooth = half - half * sine
        smooth_slope = half * cosine * (-math.pi / cutoff_radius)
        radial = []
        slope = []
        for center in radial_centers:
            away = (distance - center) * (1.0 / radial_width)
            bell = jnp.exp(-away * away)
            radial.append(smooth * bell)
            slope.append(bell * (smooth_slope - smooth * away * (2.0 / radial_width)))
        radials.append(radial)
        slopes.append(slope)

    scaled = [
        [
            [direction[axis] * (1.0 / power) if power > 1 else direction[axis] for power in range(1, degrees)]
            for axis in range(3)
        ]
        for direction in directions
    ]
    monomials = {}
    kinds = len(radial_centers)
    moments = {}
    for number, triple in enumerate(exponents):
        p, q, w = triple
        if p + q + w == 0:
            monomials[triple] = None
        else:
            axis = 0 if p else (1 if q else 2)
            lower = tuple(v - (1 if a == axis else 0) for a, v in enumerate(triple))
            values = []
            for group in range(groups):
                factor = scaled[group][axis][triple[axis] - 1]
                before = monomials[lower]
                values.append(factor if before is None else before[group] * factor)
            monomials[triple] = values
        for kind in range(kinds):
            total = None
            for group in range(groups):
                term = radials[group][kind]
                if monomials[triple] is not None:
                    term = term * monomials[triple][group]
                total = term if total is None else total + term
            moments[kind, triple] = over_group(total)

    weighted = {}
    for triple in exponents:
        weight = moment_scale**2 * math.factorial(sum(triple))
        for power in triple:
            weight *= math.factorial(power)
        for kind in range(kinds):
            weighted[kind, triple] = moments[kind, triple] * weight
    descriptor = []
    for first, second in pair_list:
        for degree in range(degrees):
            total = None
            for triple in exponents:
                if sum(triple) == degree:
                    term = weighted[first, triple] * moments[second, triple]
                    total = term if total is None else total + term
            descriptor.append(total)
    count = len(descriptor)
    padded = packed.shape[1] // 8 * per_group
    for start in range(0, padded, per_group):
        out = descriptor[min(start, count - 1)]
        for number in range(1, per_group):
            out = jnp.where(which == number, descriptor[min(start + number, count - 1)], out)
        packed[0, start * halves : start * halves + 8, :] = out
    matrix = alpha[...]
    matrix = 0.5 * (matrix + matrix.T)
    eye = lax.broadcasted_iota(jnp.int32, (count, count), 0) == lax.broadcasted_iota(
        jnp.int32, (count, count), 1
    )
    linear = jnp.sum(jnp.where(eye, jnp.broadcast_to(beta[...], (count, count)), 0.0), axis=1, keepdims=True)
    features = jnp.concatenate(
        [packed[0, pl.ds(number, count, stride=halves), :] for number in range(halves)], axis=1
    )
    slope = linear + lax.dot_general(
        matrix, features, (((1,), (0,)), ((), ())), precision=highest, preferred_element_type=f32
    )
    energy_out[...] = 0.5 * jnp.sum(features * (linear + slope), axis=0, keepdims=True)
    for number in range(halves):
        packed[1, pl.ds(number, count, stride=halves), :] = slope[:, lanes * number : lanes * (number + 1)]

    sensitivities = []
    for number in range(count):
        sensitivities.append(
            by_half([packed[1, number * halves + h : number * halves + h + 1, :] for h in range(halves)])
        )
    backs = {}
    for triple in exponents:
        degree = sum(triple)
        for kind in range(kinds):
            total = None
            for place, (first, second) in enumerate(pair_list):
                if kind not in (first, second):
                    continue
                other = second if kind == first else first
                term = sensitivities[place * degrees + degree]
                if first == second:
                    term = term + term
                term = term * weighted[other, triple]
                total = term if total is None else total + term
            backs[kind, triple] = total

    sums = [None] * 3
    for group in range(groups):
        along = None
        tangent = [None] * 3
        for triple in exponents:
            mono = None if sum(triple) == 0 else monomials[triple][group]
            weight = None
            rise = None
            for kind in range(kinds):
                back = backs[kind, triple]
                term = slopes[group][kind] * back
                rise = term if rise is None else rise + term
                if mono is not None:
                    term = radials[group][kind] * back
                    weight = term if weight is None else weight + term
            if mono is not None:
                rise = rise * mono
            along = rise if along is None else along + rise
            if mono is None:
                continue
            for axis in range(3):
                if triple[axis] == 0:
                    continue
                lower = tuple(v - (1 if a == axis else 0) for a, v in enumerate(triple))
                term = weight if monomials[lower] is None else weight * monomials[lower][group]
                tangent[axis] = term if tangent[axis] is None else tangent[axis] + term
        direction = directions[group]
        radial_part = (
            direction[0] * tangent[0] + direction[1] * tangent[1] + direction[2] * tangent[2]
        )
        straight = along - radial_part * inverses[group]
        for axis in range(3):
            gradient = direction[axis] * straight + tangent[axis] * inverses[group]
            grads[axis, 8 * group : 8 * group + 8, :] = gradient
            sums[axis] = gradient if sums[axis] is None else sums[axis] + gradient

    items = []
    for row in range(neighbours * halves):
        value = jnp.where(
            (sub == 0) | (sub == 3),
            rows_of(grads[0, row : row + 1, :]),
            jnp.where(
                (sub == 1) | (sub == 4),
                rows_of(grads[1, row : row + 1, :]),
                rows_of(grads[2, row : row + 1, :]),
            ),
        )
        spot = spots[row : row + 1, :]
        items.append((value, spot & (lanes - 1), spot >> 7))
    product = scatter_product(items, block_count)
    totals = [over_group(value) for value in sums]
    for number in range(own_blocks):
        self_part = jnp.concatenate([totals[axis][number : number + 1] for axis in range(3)], axis=0)
        own_out[:, lanes * number : lanes * (number + 1)] = summed(product, number) - self_part
    trans_out[...] = summed(product, own_blocks)
    lower_out[...] = summed(product, own_blocks + 1)
    upper_out[...] = summed(product, own_blocks + 2)


def shock_back_kernel(own, trans, back_lower, back_upper, shock_send, own_out, trans_out):
    own_blocks = own.shape[1] // lanes
    width = trans_out.shape[2]
    items = []
    for way, back in enumerate((back_lower, back_upper)):
        spot = shock_send[way : way + 1, :]
        items.append((twice(back[...]), spot & (lanes - 1), spot >> 7))
    product = scatter_product(items, own_blocks + 1)
    for number in range(own_blocks):
        cut = slice(lanes * number, lanes * (number + 1))
        own_out[:, cut] = own[:, cut] + summed(product, number)
    ghosts = trans[...] + summed(product, own_blocks)
    trans_out[0] = ghosts[:, :width]
    trans_out[1] = ghosts[:, width : 2 * width]


def final_kernel(
    live_count,
    leaving_count,
    leaving_scalars,
    disp,
    vel,
    force,
    displaced,
    own,
    back,
    trans_send,
    energy,
    leaving_slots,
    disp_out,
    vel_out,
    force_out,
    energy_out,
    payload_out,
):
    own_blocks = own.shape[1] // lanes
    items = []
    for way in range(2):
        spot = pad_lanes(trans_send[way : way + 1, :], -1)
        items.append((twice(pad_lanes(back[1 - way])), spot & (lanes - 1), spot >> 7))
    product = scatter_product(items, own_blocks)
    leaving = leaving_slots.shape[1]
    column = pad_lanes(leaving_slots[...])
    blocks = []
    for number in range(own_blocks):
        cut = slice(lanes * number, lanes * (number + 1))
        new_force = -(own[:, cut] + summed(product, number))
        new_velocity = (vel[:, cut] + kick_factor * force[:, cut]) + kick_factor * new_force
        place = displaced[:, cut]
        slot = lax.broadcasted_iota(jnp.int32, (1, lanes), 1) + lanes * number
        keep = slot < live_count[0]
        for entry in range(leaving):
            target = jnp.where(entry < leaving_count[0], leaving_scalars[entry], -1)
            keep = keep & (slot != target)
        kept = jnp.where(keep, 1.0, 0.0)
        disp_out[:, cut] = place * kept
        vel_out[:, cut] = new_velocity * kept
        force_out[:, cut] = new_force * kept
        energy_out[:, cut] = energy[:, cut] * kept
        blocks.append(jnp.concatenate([pad_rows(place), pad_rows(new_velocity), pad_rows(new_force)], axis=0))
    picked = pick_columns(blocks, column)
    sending = lax.broadcasted_iota(jnp.int32, picked.shape, 1) < leaving_count[0]
    picked = jnp.where(sending, picked, 0.0)
    for number in range(3):
        payload_out[number] = picked[8 * number : 8 * number + 3, :leaving]


def along_shock(x, by):
    devices = lax.axis_size("shock")
    return lax.ppermute(
        x, "shock", [(i, i + by) for i in range(devices) if 0 <= i + by < devices]
    )


def across(x):
    devices = lax.axis_size("trans")
    down = [(i, (i - 1) % devices) for i in range(devices)]
    up = [(i, (i + 1) % devices) for i in range(devices)]
    if sorted(down) == sorted(up):
        return lax.ppermute(x, "trans", down)
    return jnp.stack([lax.ppermute(x[0], "trans", down), lax.ppermute(x[1], "trans", up)])


def shaped(*dims):
    return jax.ShapeDtypeStruct(dims, f32)


def shards(
    displacement,
    velocity,
    force_before,
    beta,
    alpha,
    live_count,
    trans_send,
    shock_send,
    neighbour_block,
    neighbour_lane,
    leaving_slots,
    leaving_count,
):
    slots = displacement.shape[1]
    trans_width = trans_send.shape[1]
    shock_width = shock_send.shape[1]
    neighbours = neighbour_block.shape[0]
    leaving = leaving_slots.shape[0]
    halves = slots // lanes
    groups = -(-neighbours // (8 // halves))
    count = len(pair_list) * degrees
    assert slots % lanes == 0 and 8 % halves == 0 and halves <= 4
    assert shock_width == lanes and 2 * trans_width <= lanes
    displaced, trans_go = pl.pallas_call(
        start_kernel,
        out_shape=(shaped(3, slots), shaped(2, 3, trans_width)),
        name="start",
    )(displacement, velocity, force_before, trans_send)
    trans_in = across(trans_go)
    to_lower, to_upper = pl.pallas_call(
        shock_kernel,
        out_shape=(shaped(3, shock_width), shaped(3, shock_width)),
        scratch_shapes=[pltpu.VMEM((8, lanes), f32)],
        name="shock",
    )(displaced, trans_in, shock_send)
    from_lower = along_shock(to_upper, 1)
    from_upper = along_shock(to_lower, -1)
    packed_rows = -(-(count * halves) // 8) * 8
    energy, own, trans, lower, upper = pl.pallas_call(
        energy_kernel,
        out_shape=(
            shaped(1, slots),
            shaped(3, slots),
            shaped(3, lanes),
            shaped(3, lanes),
            shaped(3, lanes),
        ),
        scratch_shapes=[
            pltpu.VMEM((8, lanes), f32),
            pltpu.VMEM((groups * 8, lanes), jnp.int32),
            pltpu.VMEM((3, groups * 8, lanes), f32),
            pltpu.VMEM((2, packed_rows, lanes), f32),
            pltpu.VMEM((8, lanes), f32),
            pltpu.VMEM((8, lanes), f32),
        ],
        name="energy",
    )(
        displaced,
        trans_in,
        from_lower,
        from_upper,
        neighbour_block,
        neighbour_lane,
        beta.reshape(1, count),
        alpha,
    )
    back_lower = along_shock(upper, 1)
    back_upper = along_shock(lower, -1)
    own, trans_go = pl.pallas_call(
        shock_back_kernel,
        out_shape=(shaped(3, slots), shaped(2, 3, trans_width)),
        name="shock_back",
    )(own, trans, back_lower, back_upper, shock_send)
    back = across(trans_go)
    smem = pl.BlockSpec(memory_space=pltpu.SMEM)
    vmem = pl.BlockSpec(memory_space=pltpu.VMEM)
    disp_next, vel_next, force_next, energy, payload = pl.pallas_call(
        final_kernel,
        in_specs=[smem] * 3 + [vmem] * 9,
        out_shape=(
            shaped(3, slots),
            shaped(3, slots),
            shaped(3, slots),
            shaped(1, slots),
            shaped(3, 3, leaving),
        ),
        name="final",
    )(
        live_count,
        leaving_count,
        leaving_slots,
        displacement,
        velocity,
        force_before,
        displaced,
        own,
        back,
        trans_send,
        energy,
        leaving_slots.reshape(1, leaving),
    )
    arrivals = along_shock(payload, -1)
    return (disp_next, vel_next, force_next, energy.reshape(slots), arrivals)


def solution(mesh):
    both = ("shock", "trans")
    in_specs = (
        P(None, both),
        P(None, both),
        P(None, both),
        P(),
        P(),
        P(both),
        P(None, both),
        P(None, both),
        P(None, both),
        P(None, both),
        P(both),
        P(both),
    )
    out_specs = (P(None, both), P(None, both), P(None, both), P(both), P(None, None, both))
    return jax.shard_map(shards, mesh=mesh, in_specs=in_specs, out_specs=out_specs, check_vma=False)
```

```python
import math

import jax
import jax.numpy as jnp
import numpy as np
from jax import lax
from jax.experimental import pallas as pl
from jax.experimental.pallas import tpu as pltpu
from jax.sharding import PartitionSpec as P

kick_factor = 0.5
drift_step = 0.02
cutoff_radius = 4.2
radial_width = 0.35
radial_centers = (1.4, 1.9, 2.4, 2.9)
moment_scale = 0.25
pair_list = ((0, 0), (0, 1), (0, 2), (0, 3), (1, 1), (1, 2), (1, 3), (2, 2), (2, 3), (3, 3))
degrees = 5
lanes = 128
highest = lax.Precision.HIGHEST
f32 = jnp.float32
bf16 = jnp.bfloat16


def lattice_list():
    entries = []
    for number in range(8):
        entries.append(
            (1.0 - 2.0 * (number >> 2 & 1), 1.0 - 2.0 * (number >> 1 & 1), 1.0 - 2.0 * (number & 1))
        )
    for axis_pick in range(3):
        for signed in (2.0, -2.0):
            vector = [0.0, 0.0, 0.0]
            vector[axis_pick] = signed
            entries.append(tuple(vector))
    for zero_pick in (2, 1, 0):
        others = [axis_pick for axis_pick in range(3) if axis_pick != zero_pick]
        for leading in (2.0, -2.0):
            for trailing in (2.0, -2.0):
                vector = [0.0, 0.0, 0.0]
                vector[others[0]] = leading
                vector[others[1]] = trailing
                entries.append(tuple(vector))
    return entries


def exponent_list():
    return [
        (p, q, degree - p - q)
        for degree in range(degrees)
        for p in range(degree, -1, -1)
        for q in range(degree - p, -1, -1)
    ]


exponents = exponent_list()


def rows_of(value, count=8):
    return jnp.broadcast_to(value, (count,) + value.shape[1:])


def pick_lanes(table, index):
    return jnp.take_along_axis(table, index, axis=1, mode="promise_in_bounds")


def pick_columns(blocks, column):
    rows = blocks[0].shape[0]
    lane = rows_of(column & (lanes - 1), rows)
    block = rows_of(column >> 7, rows)
    out = jnp.zeros((rows, lanes), f32)
    for number, table in enumerate(blocks):
        out = jnp.where(block == number, pick_lanes(table, lane), out)
    return out


def pad_lanes(value, fill=0):
    rows, width = value.shape
    if width == lanes:
        return value
    return jnp.concatenate([value, jnp.full((rows, lanes - width), fill, value.dtype)], axis=1)


def pad_rows(value, count=8):
    rows = value.shape[0]
    return jnp.concatenate([value, jnp.zeros((count - rows,) + value.shape[1:], value.dtype)], axis=0)


def scatter_product(items, block_count):
    sub = lax.broadcasted_iota(jnp.int32, (8, lanes), 0)
    spot = lax.broadcasted_iota(jnp.int32, (lanes, lanes), 0)
    left = []
    right = []
    for value, lane, block in items:
        high = value.astype(bf16).astype(f32)
        part = jnp.where(sub < 3, high, value - high)
        block = rows_of(block)
        left.append(
            jnp.concatenate(
                [jnp.where(block == number, part, 0.0) for number in range(block_count)], axis=0
            ).astype(bf16)
        )
        right.append(
            jnp.where(spot == jnp.broadcast_to(lane, (lanes, lanes)), 1.0, 0.0).astype(bf16)
        )
    return lax.dot_general(
        jnp.concatenate(left, axis=1),
        jnp.concatenate(right, axis=1),
        (((1,), (1,)), ((), ())),
        preferred_element_type=f32,
    )


def twice(value):
    return jnp.concatenate([value, value, value[:2]], axis=0)


def summed(product, number):
    return product[8 * number : 8 * number + 3] + product[8 * number + 3 : 8 * number + 6]


def start_kernel(disp, vel, force, trans_send, displaced_out, trans_out):
    displaced = disp[...] + drift_step * (vel[...] + kick_factor * force[...])
    displaced_out[...] = displaced
    width = trans_send.shape[1]
    blocks = [
        pad_rows(displaced[:, lanes * b : lanes * (b + 1)]) for b in range(displaced.shape[1] // lanes)
    ]
    for way in range(2):
        column = pad_lanes(trans_send[way : way + 1, :])
        trans_out[way] = pick_columns(blocks, column)[:3, :width]


def shock_kernel(displaced, trans_in, shock_send, lower_out, upper_out, trans_block):
    width = trans_in.shape[2]
    trans_block[...] = jnp.zeros(trans_block.shape, f32)
    trans_block[:3, :width] = trans_in[1]
    trans_block[:3, width : 2 * width] = trans_in[0]
    blocks = [
        pad_rows(displaced[:, lanes * b : lanes * (b + 1)]) for b in range(displaced.shape[1] // lanes)
    ]
    blocks.append(trans_block[...])
    for way, out in enumerate((lower_out, upper_out)):
        out[...] = pick_columns(blocks, shock_send[way : way + 1, :])[:3]


def energy_kernel(
    displaced,
    trans_in,
    from_lower,
    from_upper,
    neighbour_block,
    neighbour_lane,
    beta,
    alpha,
    energy_out,
    own_out,
    trans_out,
    lower_out,
    upper_out,
    trans_block,
    spots,
    grads,
    packed,
    mono_store,
    grad_store,
):
    neighbours = neighbour_block.shape[0]
    slots = displaced.shape[1]
    width = trans_in.shape[2]
    halves = slots // lanes
    per_group = 8 // halves
    groups = -(-neighbours // per_group)
    own_blocks = halves
    block_count = own_blocks + 3
    sub = lax.broadcasted_iota(jnp.int32, (8, lanes), 0)
    half_of = sub % halves
    which = sub // halves

    def by_half(pieces):
        out = rows_of(pieces[0])
        for number in range(1, halves):
            out = jnp.where(half_of == number, rows_of(pieces[number]), out)
        return out

    def by_which(values):
        out = jnp.full((8, lanes), values[0], f32)
        for number in range(1, per_group):
            if any(v != values[0] for v in values):
                out = jnp.where(which == number, values[number], out)
        return out

    def over_group(value):
        shift = 4
        while shift >= halves:
            value = value + pltpu.roll(value, shift, 0)
            shift //= 2
        return value

    column = neighbour_block[...] * lanes + neighbour_lane[...]
    column = jnp.where(column >= slots + 2 * width, column + (lanes - 2 * width), column)
    column = jnp.where(neighbour_block[...] < 0, -1, column)
    spots[...] = jnp.full(spots.shape, -1, jnp.int32)
    for number in range(halves):
        spots[pl.ds(number, neighbours, stride=halves), :] = column[
            :, lanes * number : lanes * (number + 1)
        ]
    trans_block[...] = jnp.zeros(trans_block.shape, f32)
    trans_block[:3, :width] = trans_in[1]
    trans_block[:3, width : 2 * width] = trans_in[0]

    def table(axis):
        pieces = [displaced[axis : axis + 1, lanes * b : lanes * (b + 1)] for b in range(own_blocks)]
        pieces.append(trans_block[axis : axis + 1, :])
        pieces.append(from_lower[axis : axis + 1, :])
        pieces.append(from_upper[axis : axis + 1, :])
        return pieces

    tables = [table(axis) for axis in range(3)]
    own = [by_half(tables[axis][:own_blocks]) for axis in range(3)]
    spread = [[rows_of(piece) for piece in tables[axis]] for axis in range(3)]
    offsets = lattice_list()
    offsets = offsets + [offsets[0]] * (groups * per_group - neighbours)

    directions = []
    radials = []
    slopes = []
    inverses = []
    for group in range(groups):
        spot = spots[8 * group : 8 * group + 8, :]
        live = spot >= 0
        lane = jnp.where(live, spot & (lanes - 1), 0)
        block = jnp.where(live, spot >> 7, 0)
        vector = []
        for axis in range(3):
            picked = pick_lanes(spread[axis][0], lane)
            for number in range(1, block_count):
                picked = jnp.where(block == number, pick_lanes(spread[axis][number], lane), picked)
            offset = by_which([offsets[per_group * group + i][axis] for i in range(per_group)])
            vector.append(offset + picked - own[axis])
        square = vector[0] * vector[0] + vector[1] * vector[1] + vector[2] * vector[2]
        inverse = lax.rsqrt(square)
        distance = square * inverse
        directions.append([v * inverse for v in vector])
        inverses.append(inverse)
        angle = distance * (math.pi / cutoff_radius) - (math.pi / 2)
        squared = angle * angle
        sine = jnp.full_like(angle, -1.0 / math.factorial(15))
        for order in (13, 11, 9, 7, 5, 3, 1):
            sine = sine * squared + ((-1.0) ** ((order - 1) // 2)) / math.factorial(order)
        sine = sine * angle
        cosine = jnp.full_like(angle, 1.0 / math.factorial(16))
        for order in (14, 12, 10, 8, 6, 4, 2, 0):
            cosine = cosine * squared + ((-1.0) ** (order // 2)) / math.factorial(order)
        half = jnp.where(live, 0.5, 0.0)
        smooth = half - half * sine
        smooth_slope = half * cosine * (-math.pi / cutoff_radius)
        radial = []
        slope = []
        for center in radial_centers:
            away = (distance - center) * (1.0 / radial_width)
            bell = jnp.exp(-away * away)
            radial.append(smooth * bell)
            slope.append(bell * (smooth_slope - smooth * away * (2.0 / radial_width)))
        radials.append(radial)
        slopes.append(slope)

    scaled = [
        [
            [direction[axis] * (1.0 / power) if power > 1 else direction[axis] for power in range(1, degrees)]
            for axis in range(3)
        ]
        for direction in directions
    ]
    monomials = {}
    kinds = len(radial_centers)
    moments = {}
    for number, triple in enumerate(exponents):
        p, q, w = triple
        if p + q + w == 0:
            monomials[triple] = None
        else:
            axis = 0 if p else (1 if q else 2)
            lower = tuple(v - (1 if a == axis else 0) for a, v in enumerate(triple))
            values = []
            for group in range(groups):
                factor = scaled[group][axis][triple[axis] - 1]
                before = monomials[lower]
                values.append(factor if before is None else before[group] * factor)
            monomials[triple] = values
        for kind in range(kinds):
            total = None
            for group in range(groups):
                term = radials[group][kind]
                if monomials[triple] is not None:
                    term = term * monomials[triple][group]
                total = term if total is None else total + term
            moments[kind, triple] = over_group(total)

    weighted = {}
    for triple in exponents:
        weight = moment_scale**2 * math.factorial(sum(triple))
        for power in triple:
            weight *= math.factorial(power)
        for kind in range(kinds):
            weighted[kind, triple] = moments[kind, triple] * weight
    descriptor = []
    for first, second in pair_list:
        for degree in range(degrees):
            total = None
            for triple in exponents:
                if sum(triple) == degree:
                    term = weighted[first, triple] * moments[second, triple]
                    total = term if total is None else total + term
            descriptor.append(total)
    count = len(descriptor)
    padded = packed.shape[1] // 8 * per_group
    for start in range(0, padded, per_group):
        out = descriptor[min(start, count - 1)]
        for number in range(1, per_group):
            out = jnp.where(which == number, descriptor[min(start + number, count - 1)], out)
        packed[0, start * halves : start * halves + 8, :] = out
    matrix = alpha[...]
    matrix = 0.5 * (matrix + matrix.T)
    eye = lax.broadcasted_iota(jnp.int32, (count, count), 0) == lax.broadcasted_iota(
        jnp.int32, (count, count), 1
    )
    linear = jnp.sum(jnp.where(eye, jnp.broadcast_to(beta[...], (count, count)), 0.0), axis=1, keepdims=True)
    features = jnp.concatenate(
        [packed[0, pl.ds(number, count, stride=halves), :] for number in range(halves)], axis=1
    )
    slope = linear + lax.dot_general(
        matrix, features, (((1,), (0,)), ((), ())), precision=highest, preferred_element_type=f32
    )
    energy_out[...] = 0.5 * jnp.sum(features * (linear + slope), axis=0, keepdims=True)
    for number in range(halves):
        packed[1, pl.ds(number, count, stride=halves), :] = slope[:, lanes * number : lanes * (number + 1)]

    sensitivities = []
    for number in range(count):
        sensitivities.append(
            by_half([packed[1, number * halves + h : number * halves + h + 1, :] for h in range(halves)])
        )
    backs = {}
    for triple in exponents:
        degree = sum(triple)
        for kind in range(kinds):
            total = None
            for place, (first, second) in enumerate(pair_list):
                if kind not in (first, second):
                    continue
                other = second if kind == first else first
                term = sensitivities[place * degrees + degree]
                if first == second:
                    term = term + term
                term = term * weighted[other, triple]
                total = term if total is None else total + term
            backs[kind, triple] = total

    sums = [None] * 3
    for group in range(groups):
        along = None
        tangent = [None] * 3
        for triple in exponents:
            mono = None if sum(triple) == 0 else monomials[triple][group]
            weight = None
            rise = None
            for kind in range(kinds):
                back = backs[kind, triple]
                term = slopes[group][kind] * back
                rise = term if rise is None else rise + term
                if mono is not None:
                    term = radials[group][kind] * back
                    weight = term if weight is None else weight + term
            if mono is not None:
                rise = rise * mono
            along = rise if along is None else along + rise
            if mono is None:
                continue
            for axis in range(3):
                if triple[axis] == 0:
                    continue
                lower = tuple(v - (1 if a == axis else 0) for a, v in enumerate(triple))
                term = weight if monomials[lower] is None else weight * monomials[lower][group]
                tangent[axis] = term if tangent[axis] is None else tangent[axis] + term
        direction = directions[group]
        radial_part = (
            direction[0] * tangent[0] + direction[1] * tangent[1] + direction[2] * tangent[2]
        )
        straight = along - radial_part * inverses[group]
        for axis in range(3):
            gradient = direction[axis] * straight + tangent[axis] * inverses[group]
            grads[axis, 8 * group : 8 * group + 8, :] = gradient
            sums[axis] = gradient if sums[axis] is None else sums[axis] + gradient

    items = []
    for row in range(neighbours * halves):
        value = jnp.where(
            (sub == 0) | (sub == 3),
            rows_of(grads[0, row : row + 1, :]),
            jnp.where(
                (sub == 1) | (sub == 4),
                rows_of(grads[1, row : row + 1, :]),
                rows_of(grads[2, row : row + 1, :]),
            ),
        )
        spot = spots[row : row + 1, :]
        items.append((value, spot & (lanes - 1), spot >> 7))
    product = scatter_product(items, block_count)
    totals = [over_group(value) for value in sums]
    for number in range(own_blocks):
        self_part = jnp.concatenate([totals[axis][number : number + 1] for axis in range(3)], axis=0)
        own_out[:, lanes * number : lanes * (number + 1)] = summed(product, number) - self_part
    trans_out[...] = summed(product, own_blocks)
    lower_out[...] = summed(product, own_blocks + 1)
    upper_out[...] = summed(product, own_blocks + 2)


def shock_back_kernel(own, trans, back_lower, back_upper, shock_send, own_out, trans_out):
    own_blocks = own.shape[1] // lanes
    width = trans_out.shape[2]
    items = []
    for way, back in enumerate((back_lower, back_upper)):
        spot = shock_send[way : way + 1, :]
        items.append((twice(back[...]), spot & (lanes - 1), spot >> 7))
    product = scatter_product(items, own_blocks + 1)
    for number in range(own_blocks):
        cut = slice(lanes * number, lanes * (number + 1))
        own_out[:, cut] = own[:, cut] + summed(product, number)
    ghosts = trans[...] + summed(product, own_blocks)
    trans_out[0] = ghosts[:, :width]
    trans_out[1] = ghosts[:, width : 2 * width]


def final_kernel(
    live_count,
    leaving_count,
    leaving_scalars,
    disp,
    vel,
    force,
    displaced,
    own,
    back,
    trans_send,
    energy,
    leaving_slots,
    disp_out,
    vel_out,
    force_out,
    energy_out,
    payload_out,
):
    own_blocks = own.shape[1] // lanes
    items = []
    for way in range(2):
        spot = pad_lanes(trans_send[way : way + 1, :], -1)
        items.append((twice(pad_lanes(back[1 - way])), spot & (lanes - 1), spot >> 7))
    product = scatter_product(items, own_blocks)
    leaving = leaving_slots.shape[1]
    column = pad_lanes(leaving_slots[...])
    blocks = []
    for number in range(own_blocks):
        cut = slice(lanes * number, lanes * (number + 1))
        new_force = -(own[:, cut] + summed(product, number))
        new_velocity = (vel[:, cut] + kick_factor * force[:, cut]) + kick_factor * new_force
        place = displaced[:, cut]
        slot = lax.broadcasted_iota(jnp.int32, (1, lanes), 1) + lanes * number
        keep = slot < live_count[0]
        for entry in range(leaving):
            target = jnp.where(entry < leaving_count[0], leaving_scalars[entry], -1)
            keep = keep & (slot != target)
        kept = jnp.where(keep, 1.0, 0.0)
        disp_out[:, cut] = place * kept
        vel_out[:, cut] = new_velocity * kept
        force_out[:, cut] = new_force * kept
        energy_out[:, cut] = energy[:, cut] * kept
        blocks.append(jnp.concatenate([pad_rows(place), pad_rows(new_velocity), pad_rows(new_force)], axis=0))
    picked = pick_columns(blocks, column)
    sending = lax.broadcasted_iota(jnp.int32, picked.shape, 1) < leaving_count[0]
    picked = jnp.where(sending, picked, 0.0)
    for number in range(3):
        payload_out[number] = picked[8 * number : 8 * number + 3, :leaving]


def along_shock(x, by):
    devices = lax.axis_size("shock")
    return lax.ppermute(
        x, "shock", [(i, i + by) for i in range(devices) if 0 <= i + by < devices]
    )


def around_shock(x, by):
    devices = lax.axis_size("shock")
    return lax.ppermute(x, "shock", [(i, (i + by) % devices) for i in range(devices)])


def across(x):
    devices = lax.axis_size("trans")
    down = [(i, (i - 1) % devices) for i in range(devices)]
    up = [(i, (i + 1) % devices) for i in range(devices)]
    if sorted(down) == sorted(up):
        return lax.ppermute(x, "trans", down)
    return jnp.stack([lax.ppermute(x[0], "trans", down), lax.ppermute(x[1], "trans", up)])


def shaped(*dims):
    return jax.ShapeDtypeStruct(dims, f32)


def shards(
    displacement,
    velocity,
    force_before,
    beta,
    alpha,
    live_count,
    trans_send,
    shock_send,
    neighbour_block,
    neighbour_lane,
    leaving_slots,
    leaving_count,
):
    slots = displacement.shape[1]
    trans_width = trans_send.shape[1]
    shock_width = shock_send.shape[1]
    neighbours = neighbour_block.shape[0]
    leaving = leaving_slots.shape[0]
    halves = slots // lanes
    groups = -(-neighbours // (8 // halves))
    count = len(pair_list) * degrees
    assert slots % lanes == 0 and 8 % halves == 0 and halves <= 4
    assert shock_width == lanes and 2 * trans_width <= lanes
    displaced, trans_go = pl.pallas_call(
        start_kernel,
        out_shape=(shaped(3, slots), shaped(2, 3, trans_width)),
        name="start",
    )(displacement, velocity, force_before, trans_send)
    trans_in = across(trans_go)
    to_lower, to_upper = pl.pallas_call(
        shock_kernel,
        out_shape=(shaped(3, shock_width), shaped(3, shock_width)),
        scratch_shapes=[pltpu.VMEM((8, lanes), f32)],
        name="shock",
    )(displaced, trans_in, shock_send)
    from_lower = around_shock(to_upper, 1)
    from_upper = around_shock(to_lower, -1)
    packed_rows = -(-(count * halves) // 8) * 8
    energy, own, trans, lower, upper = pl.pallas_call(
        energy_kernel,
        out_shape=(
            shaped(1, slots),
            shaped(3, slots),
            shaped(3, lanes),
            shaped(3, lanes),
            shaped(3, lanes),
        ),
        scratch_shapes=[
            pltpu.VMEM((8, lanes), f32),
            pltpu.VMEM((groups * 8, lanes), jnp.int32),
            pltpu.VMEM((3, groups * 8, lanes), f32),
            pltpu.VMEM((2, packed_rows, lanes), f32),
            pltpu.VMEM((8, lanes), f32),
            pltpu.VMEM((8, lanes), f32),
        ],
        name="energy",
    )(
        displaced,
        trans_in,
        from_lower,
        from_upper,
        neighbour_block,
        neighbour_lane,
        beta.reshape(1, count),
        alpha,
    )
    back_lower = around_shock(upper, 1)
    back_upper = around_shock(lower, -1)
    own, trans_go = pl.pallas_call(
        shock_back_kernel,
        out_shape=(shaped(3, slots), shaped(2, 3, trans_width)),
        name="shock_back",
    )(own, trans, back_lower, back_upper, shock_send)
    back = across(trans_go)
    smem = pl.BlockSpec(memory_space=pltpu.SMEM)
    vmem = pl.BlockSpec(memory_space=pltpu.VMEM)
    disp_next, vel_next, force_next, energy, payload = pl.pallas_call(
        final_kernel,
        in_specs=[smem] * 3 + [vmem] * 9,
        out_shape=(
            shaped(3, slots),
            shaped(3, slots),
            shaped(3, slots),
            shaped(1, slots),
            shaped(3, 3, leaving),
        ),
        name="final",
    )(
        live_count,
        leaving_count,
        leaving_slots,
        displacement,
        velocity,
        force_before,
        displaced,
        own,
        back,
        trans_send,
        energy,
        leaving_slots.reshape(1, leaving),
    )
    arrivals = along_shock(payload, -1)
    return (disp_next, vel_next, force_next, energy.reshape(slots), arrivals)


def solution(mesh):
    both = ("shock", "trans")
    in_specs = (
        P(None, both),
        P(None, both),
        P(None, both),
        P(),
        P(),
        P(both),
        P(None, both),
        P(None, both),
        P(None, both),
        P(None, both),
        P(both),
        P(both),
    )
    out_specs = (P(None, both), P(None, both), P(None, both), P(both), P(None, None, both))
    return jax.shard_map(shards, mesh=mesh, in_specs=in_specs, out_specs=out_specs, check_vma=False)
```

```python
import math

import jax
import jax.numpy as jnp
import numpy as np
from jax import lax
from jax.experimental import pallas as pl
from jax.experimental.pallas import tpu as pltpu
from jax.sharding import PartitionSpec as P

kick_factor = 0.5
drift_step = 0.02
cutoff_radius = 4.2
radial_width = 0.35
radial_centers = (1.4, 1.9, 2.4, 2.9)
moment_scale = 0.25
pair_list = ((0, 0), (0, 1), (0, 2), (0, 3), (1, 1), (1, 2), (1, 3), (2, 2), (2, 3), (3, 3))
degrees = 5
lanes = 128
highest = lax.Precision.HIGHEST
f32 = jnp.float32
bf16 = jnp.bfloat16


def lattice_list():
    entries = []
    for number in range(8):
        entries.append(
            (1.0 - 2.0 * (number >> 2 & 1), 1.0 - 2.0 * (number >> 1 & 1), 1.0 - 2.0 * (number & 1))
        )
    for axis_pick in range(3):
        for signed in (2.0, -2.0):
            vector = [0.0, 0.0, 0.0]
            vector[axis_pick] = signed
            entries.append(tuple(vector))
    for zero_pick in (2, 1, 0):
        others = [axis_pick for axis_pick in range(3) if axis_pick != zero_pick]
        for leading in (2.0, -2.0):
            for trailing in (2.0, -2.0):
                vector = [0.0, 0.0, 0.0]
                vector[others[0]] = leading
                vector[others[1]] = trailing
                entries.append(tuple(vector))
    return entries


def exponent_list():
    return [
        (p, q, degree - p - q)
        for degree in range(degrees)
        for p in range(degree, -1, -1)
        for q in range(degree - p, -1, -1)
    ]


exponents = exponent_list()


def rows_of(value, count=8):
    return jnp.broadcast_to(value, (count,) + value.shape[1:])


def pick_lanes(table, index):
    return jnp.take_along_axis(table, index, axis=1, mode="promise_in_bounds")


def pick_columns(blocks, column):
    rows = blocks[0].shape[0]
    lane = rows_of(column & (lanes - 1), rows)
    block = rows_of(column >> 7, rows)
    out = jnp.zeros((rows, lanes), f32)
    for number, table in enumerate(blocks):
        out = jnp.where(block == number, pick_lanes(table, lane), out)
    return out


def pad_lanes(value, fill=0):
    rows, width = value.shape
    if width == lanes:
        return value
    return jnp.concatenate([value, jnp.full((rows, lanes - width), fill, value.dtype)], axis=1)


def pad_rows(value, count=8):
    rows = value.shape[0]
    return jnp.concatenate([value, jnp.zeros((count - rows,) + value.shape[1:], value.dtype)], axis=0)


def scatter_product(items, block_count):
    sub = lax.broadcasted_iota(jnp.int32, (8, lanes), 0)
    spot = lax.broadcasted_iota(jnp.int32, (lanes, lanes), 0)
    left = []
    right = []
    for value, lane, block in items:
        high = value.astype(bf16).astype(f32)
        part = jnp.where(sub < 3, high, value - high)
        block = rows_of(block)
        left.append(
            jnp.concatenate(
                [jnp.where(block == number, part, 0.0) for number in range(block_count)], axis=0
            ).astype(bf16)
        )
        right.append(
            jnp.where(spot == jnp.broadcast_to(lane, (lanes, lanes)), 1.0, 0.0).astype(bf16)
        )
    return lax.dot_general(
        jnp.concatenate(left, axis=1),
        jnp.concatenate(right, axis=1),
        (((1,), (1,)), ((), ())),
        preferred_element_type=f32,
    )


def twice(value):
    return jnp.concatenate([value, value, value[:2]], axis=0)


def summed(product, number):
    return product[8 * number : 8 * number + 3] + product[8 * number + 3 : 8 * number + 6]


def start_kernel(disp, vel, force, trans_send, displaced_out, trans_out):
    displaced = disp[...] + drift_step * (vel[...] + kick_factor * force[...])
    displaced_out[...] = displaced
    width = trans_send.shape[1]
    blocks = [
        pad_rows(displaced[:, lanes * b : lanes * (b + 1)]) for b in range(displaced.shape[1] // lanes)
    ]
    for way in range(2):
        column = pad_lanes(trans_send[way : way + 1, :])
        trans_out[way] = pick_columns(blocks, column)[:3, :width]


def prepare_kernel(
    live_count,
    leaving_count,
    leaving_scalars,
    vel,
    force,
    trans_send,
    shock_send,
    neighbour_block,
    neighbour_lane,
    beta,
    alpha,
    leaving_slots,
    half_out,
    kept_out,
    trans_spots_out,
    shock_spots_out,
    spots_out,
    linear_out,
    matrix_out,
    leaving_out,
):
    neighbours, slots = neighbour_block.shape
    halves = slots // lanes
    width = trans_send.shape[1]
    half_out[...] = vel[...] + kick_factor * force[...]
    column = neighbour_block[...] * lanes + neighbour_lane[...]
    column = jnp.where(column >= slots + 2 * width, column + (lanes - 2 * width), column)
    column = jnp.where(neighbour_block[...] < 0, -1, column)
    spots_out[...] = jnp.full(spots_out.shape, -1, jnp.int32)
    for number in range(halves):
        spots_out[pl.ds(number, neighbours, stride=halves), :] = column[
            :, lanes * number : lanes * (number + 1)
        ]
    trans_spots_out[...] = pad_lanes(trans_send[...], -1)
    shock_spots_out[...] = shock_send[...]
    matrix = alpha[...]
    count = matrix.shape[0]
    matrix_out[...] = 0.5 * (matrix + matrix.T)
    eye = lax.broadcasted_iota(jnp.int32, (count, count), 0) == lax.broadcasted_iota(
        jnp.int32, (count, count), 1
    )
    linear = jnp.sum(
        jnp.where(eye, jnp.broadcast_to(beta[...], (count, count)), 0.0), axis=1, keepdims=True
    )
    linear_out[...] = jnp.broadcast_to(linear, linear_out.shape)
    slot = lax.broadcasted_iota(jnp.int32, (1, slots), 1)
    keep = slot < live_count[0]
    leaving = leaving_slots.shape[1]
    for entry in range(leaving):
        target = jnp.where(entry < leaving_count[0], leaving_scalars[entry], -1)
        keep = keep & (slot != target)
    kept_out[...] = jnp.where(keep, 1.0, 0.0)
    sending = lax.broadcasted_iota(jnp.int32, (1, lanes), 1) < leaving_count[0]
    leaving_out[...] = jnp.where(sending, pad_lanes(leaving_slots[...], -1), -1)


def shock_kernel(displaced, trans_in, shock_send, lower_out, upper_out, trans_block):
    width = trans_in.shape[2]
    trans_block[...] = jnp.zeros(trans_block.shape, f32)
    trans_block[:3, :width] = trans_in[1]
    trans_block[:3, width : 2 * width] = trans_in[0]
    blocks = [
        pad_rows(displaced[:, lanes * b : lanes * (b + 1)]) for b in range(displaced.shape[1] // lanes)
    ]
    blocks.append(trans_block[...])
    for way, out in enumerate((lower_out, upper_out)):
        out[...] = pick_columns(blocks, shock_send[way : way + 1, :])[:3]


def energy_kernel(
    displaced,
    trans_in,
    from_lower,
    from_upper,
    spots,
    linear,
    matrix,
    energy_out,
    own_out,
    trans_out,
    lower_out,
    upper_out,
    trans_block,
    grads,
    packed,
):
    slots = displaced.shape[1]
    width = trans_in.shape[2]
    halves = slots // lanes
    per_group = 8 // halves
    groups = spots.shape[0] // 8
    own_blocks = halves
    block_count = own_blocks + 3
    sub = lax.broadcasted_iota(jnp.int32, (8, lanes), 0)
    half_of = sub % halves
    which = sub // halves

    def by_half(pieces):
        out = rows_of(pieces[0])
        for number in range(1, halves):
            out = jnp.where(half_of == number, rows_of(pieces[number]), out)
        return out

    def by_which(values):
        out = jnp.full((8, lanes), values[0], f32)
        for number in range(1, per_group):
            if any(v != values[0] for v in values):
                out = jnp.where(which == number, values[number], out)
        return out

    def over_group(value):
        shift = 4
        while shift >= halves:
            value = value + pltpu.roll(value, shift, 0)
            shift //= 2
        return value

    trans_block[...] = jnp.zeros(trans_block.shape, f32)
    trans_block[:3, :width] = trans_in[1]
    trans_block[:3, width : 2 * width] = trans_in[0]

    def table(axis):
        pieces = [displaced[axis : axis + 1, lanes * b : lanes * (b + 1)] for b in range(own_blocks)]
        pieces.append(trans_block[axis : axis + 1, :])
        pieces.append(from_lower[axis : axis + 1, :])
        pieces.append(from_upper[axis : axis + 1, :])
        return pieces

    tables = [table(axis) for axis in range(3)]
    own = [by_half(tables[axis][:own_blocks]) for axis in range(3)]
    spread = [[rows_of(piece) for piece in tables[axis]] for axis in range(3)]
    offsets = lattice_list()
    neighbours = len(offsets)
    offsets = offsets + [offsets[0]] * (groups * per_group - neighbours)

    directions = []
    radials = []
    slopes = []
    inverses = []
    for group in range(groups):
        spot = spots[8 * group : 8 * group + 8, :]
        live = spot >= 0
        lane = jnp.where(live, spot & (lanes - 1), 0)
        block = jnp.where(live, spot >> 7, 0)
        vector = []
        for axis in range(3):
            picked = pick_lanes(spread[axis][0], lane)
            for number in range(1, block_count):
                picked = jnp.where(block == number, pick_lanes(spread[axis][number], lane), picked)
            offset = by_which([offsets[per_group * group + i][axis] for i in range(per_group)])
            vector.append(offset + picked - own[axis])
        square = vector[0] * vector[0] + vector[1] * vector[1] + vector[2] * vector[2]
        inverse = lax.rsqrt(square)
        distance = square * inverse
        directions.append([v * inverse for v in vector])
        inverses.append(inverse)
        angle = distance * (math.pi / cutoff_radius) - (math.pi / 2)
        squared = angle * angle
        sine = jnp.full_like(angle, -1.0 / math.factorial(15))
        for order in (13, 11, 9, 7, 5, 3, 1):
            sine = sine * squared + ((-1.0) ** ((order - 1) // 2)) / math.factorial(order)
        sine = sine * angle
        cosine = jnp.full_like(angle, 1.0 / math.factorial(16))
        for order in (14, 12, 10, 8, 6, 4, 2, 0):
            cosine = cosine * squared + ((-1.0) ** (order // 2)) / math.factorial(order)
        half = jnp.where(live, 0.5, 0.0)
        smooth = half - half * sine
        smooth_slope = half * cosine * (-math.pi / cutoff_radius)
        radial = []
        slope = []
        for center in radial_centers:
            away = (distance - center) * (1.0 / radial_width)
            bell = jnp.exp(-away * away)
            radial.append(smooth * bell)
            slope.append(bell * (smooth_slope - smooth * away * (2.0 / radial_width)))
        radials.append(radial)
        slopes.append(slope)

    scaled = [
        [
            [direction[axis] * (1.0 / power) if power > 1 else direction[axis] for power in range(1, degrees)]
            for axis in range(3)
        ]
        for direction in directions
    ]
    monomials = {}
    kinds = len(radial_centers)
    moments = {}
    for number, triple in enumerate(exponents):
        p, q, w = triple
        if p + q + w == 0:
            monomials[triple] = None
        else:
            axis = 0 if p else (1 if q else 2)
            lower = tuple(v - (1 if a == axis else 0) for a, v in enumerate(triple))
            values = []
            for group in range(groups):
                factor = scaled[group][axis][triple[axis] - 1]
                before = monomials[lower]
                values.append(factor if before is None else before[group] * factor)
            monomials[triple] = values
        for kind in range(kinds):
            total = None
            for group in range(groups):
                term = radials[group][kind]
                if monomials[triple] is not None:
                    term = term * monomials[triple][group]
                total = term if total is None else total + term
            moments[kind, triple] = over_group(total)

    weighted = {}
    for triple in exponents:
        weight = moment_scale**2 * math.factorial(sum(triple))
        for power in triple:
            weight *= math.factorial(power)
        for kind in range(kinds):
            weighted[kind, triple] = moments[kind, triple] * weight
    descriptor = []
    for first, second in pair_list:
        for degree in range(degrees):
            total = None
            for triple in exponents:
                if sum(triple) == degree:
                    term = weighted[first, triple] * moments[second, triple]
                    total = term if total is None else total + term
            descriptor.append(total)
    count = len(descriptor)
    padded = packed.shape[1] // 8 * per_group
    for start in range(0, padded, per_group):
        out = descriptor[min(start, count - 1)]
        for number in range(1, per_group):
            out = jnp.where(which == number, descriptor[min(start + number, count - 1)], out)
        packed[0, start * halves : start * halves + 8, :] = out
    features = jnp.concatenate(
        [packed[0, pl.ds(number, count, stride=halves), :] for number in range(halves)], axis=1
    )
    slope = linear[...] + lax.dot_general(
        matrix[...], features, (((1,), (0,)), ((), ())), precision=highest, preferred_element_type=f32
    )
    energy_out[...] = 0.5 * jnp.sum(features * (linear[...] + slope), axis=0, keepdims=True)
    for number in range(halves):
        packed[1, pl.ds(number, count, stride=halves), :] = slope[:, lanes * number : lanes * (number + 1)]

    sensitivities = []
    for number in range(count):
        sensitivities.append(
            by_half([packed[1, number * halves + h : number * halves + h + 1, :] for h in range(halves)])
        )
    backs = {}
    for triple in exponents:
        degree = sum(triple)
        for kind in range(kinds):
            total = None
            for place, (first, second) in enumerate(pair_list):
                if kind not in (first, second):
                    continue
                other = second if kind == first else first
                term = sensitivities[place * degrees + degree]
                if first == second:
                    term = term + term
                term = term * weighted[other, triple]
                total = term if total is None else total + term
            backs[kind, triple] = total

    sums = [None] * 3
    for group in range(groups):
        along = None
        tangent = [None] * 3
        for triple in exponents:
            mono = None if sum(triple) == 0 else monomials[triple][group]
            weight = None
            rise = None
            for kind in range(kinds):
                back = backs[kind, triple]
                term = slopes[group][kind] * back
                rise = term if rise is None else rise + term
                if mono is not None:
                    term = radials[group][kind] * back
                    weight = term if weight is None else weight + term
            if mono is not None:
                rise = rise * mono
            along = rise if along is None else along + rise
            if mono is None:
                continue
            for axis in range(3):
                if triple[axis] == 0:
                    continue
                lower = tuple(v - (1 if a == axis else 0) for a, v in enumerate(triple))
                term = weight if monomials[lower] is None else weight * monomials[lower][group]
                tangent[axis] = term if tangent[axis] is None else tangent[axis] + term
        direction = directions[group]
        radial_part = (
            direction[0] * tangent[0] + direction[1] * tangent[1] + direction[2] * tangent[2]
        )
        straight = along - radial_part * inverses[group]
        for axis in range(3):
            gradient = direction[axis] * straight + tangent[axis] * inverses[group]
            grads[axis, 8 * group : 8 * group + 8, :] = gradient
            sums[axis] = gradient if sums[axis] is None else sums[axis] + gradient

    items = []
    for row in range(neighbours * halves):
        value = jnp.where(
            (sub == 0) | (sub == 3),
            rows_of(grads[0, row : row + 1, :]),
            jnp.where(
                (sub == 1) | (sub == 4),
                rows_of(grads[1, row : row + 1, :]),
                rows_of(grads[2, row : row + 1, :]),
            ),
        )
        spot = spots[row : row + 1, :]
        items.append((value, spot & (lanes - 1), spot >> 7))
    product = scatter_product(items, block_count)
    totals = [over_group(value) for value in sums]
    for number in range(own_blocks):
        self_part = jnp.concatenate([totals[axis][number : number + 1] for axis in range(3)], axis=0)
        own_out[:, lanes * number : lanes * (number + 1)] = summed(product, number) - self_part
    trans_out[...] = summed(product, own_blocks)
    lower_out[...] = summed(product, own_blocks + 1)
    upper_out[...] = summed(product, own_blocks + 2)


def shock_back_kernel(own, trans, back_lower, back_upper, shock_send, own_out, trans_out):
    own_blocks = own.shape[1] // lanes
    width = trans_out.shape[2]
    items = []
    for way, back in enumerate((back_lower, back_upper)):
        spot = shock_send[way : way + 1, :]
        items.append((twice(back[...]), spot & (lanes - 1), spot >> 7))
    product = scatter_product(items, own_blocks + 1)
    for number in range(own_blocks):
        cut = slice(lanes * number, lanes * (number + 1))
        own_out[:, cut] = own[:, cut] + summed(product, number)
    ghosts = trans[...] + summed(product, own_blocks)
    trans_out[0] = ghosts[:, :width]
    trans_out[1] = ghosts[:, width : 2 * width]


def final_kernel(
    half_velocity,
    kept,
    displaced,
    own,
    back,
    trans_spots,
    energy,
    leaving_spots,
    disp_out,
    vel_out,
    force_out,
    energy_out,
    payload_out,
):
    own_blocks = own.shape[1] // lanes
    items = []
    for way in range(2):
        spot = trans_spots[way : way + 1, :]
        items.append((twice(pad_lanes(back[1 - way])), spot & (lanes - 1), spot >> 7))
    product = scatter_product(items, own_blocks)
    leaving = payload_out.shape[2]
    blocks = []
    for number in range(own_blocks):
        cut = slice(lanes * number, lanes * (number + 1))
        new_force = -(own[:, cut] + summed(product, number))
        new_velocity = half_velocity[:, cut] + kick_factor * new_force
        place = displaced[:, cut]
        keep = kept[:, cut]
        disp_out[:, cut] = place * keep
        vel_out[:, cut] = new_velocity * keep
        force_out[:, cut] = new_force * keep
        energy_out[:, cut] = energy[:, cut] * keep
        blocks.append(jnp.concatenate([pad_rows(place), pad_rows(new_velocity), pad_rows(new_force)], axis=0))
    picked = pick_columns(blocks, leaving_spots[...])
    for number in range(3):
        payload_out[number] = picked[8 * number : 8 * number + 3, :leaving]


def along_shock(x, by):
    devices = lax.axis_size("shock")
    return lax.ppermute(
        x, "shock", [(i, i + by) for i in range(devices) if 0 <= i + by < devices]
    )


def around_shock(x, by):
    devices = lax.axis_size("shock")
    return lax.ppermute(x, "shock", [(i, (i + by) % devices) for i in range(devices)])


def across(x):
    devices = lax.axis_size("trans")
    down = [(i, (i - 1) % devices) for i in range(devices)]
    up = [(i, (i + 1) % devices) for i in range(devices)]
    if sorted(down) == sorted(up):
        return lax.ppermute(x, "trans", down)
    return jnp.stack([lax.ppermute(x[0], "trans", down), lax.ppermute(x[1], "trans", up)])


def shaped(*dims, kind=f32):
    return pltpu.VMEM(dims, kind)


def run_kernel(kernel, name, out_shape, args, scratch=(), scalars=0, far=False, cost=None):
    smem = pl.BlockSpec(memory_space=pltpu.SMEM)
    vmem = pl.BlockSpec(memory_space=pltpu.VMEM)
    rest = list(args[scalars:])
    if not far:
        rest = [pltpu.with_memory_space_constraint(arg, pltpu.VMEM) for arg in rest]
    return pl.pallas_call(
        kernel,
        in_specs=[smem] * scalars + [vmem] * len(rest),
        out_specs=tuple(vmem for _ in out_shape),
        out_shape=out_shape,
        scratch_shapes=list(scratch),
        cost_estimate=cost,
        name=name,
    )(*args[:scalars], *rest)


def shards(
    displacement,
    velocity,
    force_before,
    beta,
    alpha,
    live_count,
    trans_send,
    shock_send,
    neighbour_block,
    neighbour_lane,
    leaving_slots,
    leaving_count,
):
    slots = displacement.shape[1]
    trans_width = trans_send.shape[1]
    shock_width = shock_send.shape[1]
    neighbours = neighbour_block.shape[0]
    leaving = leaving_slots.shape[0]
    halves = slots // lanes
    groups = -(-neighbours // (8 // halves))
    count = len(pair_list) * degrees
    assert slots % lanes == 0 and 8 % halves == 0 and halves <= 4
    assert shock_width == lanes and 2 * trans_width <= lanes
    displaced, trans_go = run_kernel(
        start_kernel,
        "start",
        (shaped(3, slots), shaped(2, 3, trans_width)),
        (displacement, velocity, force_before, trans_send),
        far=True,
    )
    trans_in = across(trans_go)
    whole = jnp.int32
    half_velocity, kept, trans_spots, shock_spots, spots, linear, matrix, leaving_spots = run_kernel(
        prepare_kernel,
        "prepare",
        (
            shaped(3, slots),
            shaped(1, slots),
            shaped(2, lanes, kind=whole),
            shaped(2, shock_width, kind=whole),
            shaped(groups * 8, lanes, kind=whole),
            shaped(count, slots),
            shaped(count, count),
            shaped(1, lanes, kind=whole),
        ),
        (
            live_count,
            leaving_count,
            leaving_slots,
            velocity,
            force_before,
            trans_send,
            shock_send,
            neighbour_block,
            neighbour_lane,
            beta.reshape(1, count),
            alpha,
            leaving_slots.reshape(1, leaving),
        ),
        scalars=3,
        far=True,
        cost=pl.CostEstimate(flops=40 * slots * neighbours, bytes_accessed=12 * slots * neighbours, transcendentals=0),
    )
    to_lower, to_upper = run_kernel(
        shock_kernel,
        "shock",
        (shaped(3, shock_width), shaped(3, shock_width)),
        (displaced, trans_in, shock_spots),
        (pltpu.VMEM((8, lanes), f32),),
    )
    from_lower = around_shock(to_upper, 1)
    from_upper = around_shock(to_lower, -1)
    packed_rows = -(-(count * halves) // 8) * 8
    energy, own, trans, lower, upper = run_kernel(
        energy_kernel,
        "energy",
        (shaped(1, slots), shaped(3, slots), shaped(3, lanes), shaped(3, lanes), shaped(3, lanes)),
        (displaced, trans_in, from_lower, from_upper, spots, linear, matrix),
        (
            pltpu.VMEM((8, lanes), f32),
            pltpu.VMEM((3, groups * 8, lanes), f32),
            pltpu.VMEM((2, packed_rows, lanes), f32),
        ),
    )
    back_lower = around_shock(upper, 1)
    back_upper = around_shock(lower, -1)
    own, trans_go = run_kernel(
        shock_back_kernel,
        "shock_back",
        (shaped(3, slots), shaped(2, 3, trans_width)),
        (own, trans, back_lower, back_upper, shock_spots),
    )
    back = across(trans_go)
    disp_next, vel_next, force_next, energy, payload = run_kernel(
        final_kernel,
        "final",
        (
            shaped(3, slots),
            shaped(3, slots),
            shaped(3, slots),
            shaped(1, slots),
            shaped(3, 3, leaving),
        ),
        (half_velocity, kept, displaced, own, back, trans_spots, energy, leaving_spots),
    )
    arrivals = along_shock(payload, -1)
    return (disp_next, vel_next, force_next, energy.reshape(slots), arrivals)


def solution(mesh):
    both = ("shock", "trans")
    in_specs = (
        P(None, both),
        P(None, both),
        P(None, both),
        P(),
        P(),
        P(both),
        P(None, both),
        P(None, both),
        P(None, both),
        P(None, both),
        P(both),
        P(both),
    )
    out_specs = (P(None, both), P(None, both), P(None, both), P(both), P(None, None, both))
    return jax.shard_map(shards, mesh=mesh, in_specs=in_specs, out_specs=out_specs, check_vma=False)
```

```python
import math

import jax
import jax.numpy as jnp
from jax import lax
from jax.experimental import pallas as pl
from jax.experimental.pallas import tpu as pltpu
from jax.sharding import PartitionSpec as P


kick_factor = 0.5
drift_step = 0.02
cutoff_radius = 4.2
radial_width = 0.35
radial_centers = (1.4, 1.9, 2.4, 2.9)
moment_scale = 0.25
pair_list = ((0, 0), (0, 1), (0, 2), (0, 3), (1, 1), (1, 2), (1, 3), (2, 2), (2, 3), (3, 3))
degrees = 5
lanes = 128
highest = lax.Precision.HIGHEST
f32 = jnp.float32
bf16 = jnp.bfloat16


def lattice_list():
    entries = []
    for number in range(8):
        entries.append(
            (1.0 - 2.0 * (number >> 2 & 1), 1.0 - 2.0 * (number >> 1 & 1), 1.0 - 2.0 * (number & 1))
        )
    for axis_pick in range(3):
        for signed in (2.0, -2.0):
            vector = [0.0, 0.0, 0.0]
            vector[axis_pick] = signed
            entries.append(tuple(vector))
    for zero_pick in (2, 1, 0):
        others = [axis_pick for axis_pick in range(3) if axis_pick != zero_pick]
        for leading in (2.0, -2.0):
            for trailing in (2.0, -2.0):
                vector = [0.0, 0.0, 0.0]
                vector[others[0]] = leading
                vector[others[1]] = trailing
                entries.append(tuple(vector))
    return entries


def exponent_list():
    return [
        (p, q, degree - p - q)
        for degree in range(degrees)
        for p in range(degree, -1, -1)
        for q in range(degree - p, -1, -1)
    ]


exponents = exponent_list()


def rows_of(value, count=8):
    return jnp.broadcast_to(value, (count,) + value.shape[1:])


def pick_lanes(table, index):
    return jnp.take_along_axis(table, index, axis=1, mode="promise_in_bounds")


def pick_columns(blocks, column):
    rows = blocks[0].shape[0]
    lane = rows_of(column & (lanes - 1), rows)
    block = rows_of(column >> 7, rows)
    out = jnp.zeros((rows, lanes), f32)
    for number, table in enumerate(blocks):
        out = jnp.where(block == number, pick_lanes(table, lane), out)
    return out


def pad_lanes(value, fill=0):
    rows, width = value.shape
    if width == lanes:
        return value
    return jnp.concatenate([value, jnp.full((rows, lanes - width), fill, value.dtype)], axis=1)


def pad_rows(value, count=8):
    rows = value.shape[0]
    return jnp.concatenate([value, jnp.zeros((count - rows,) + value.shape[1:], value.dtype)], axis=0)


def scatter_product(items, block_count, marks=None):
    sub = lax.broadcasted_iota(jnp.int32, (8, lanes), 0)
    spot = lax.broadcasted_iota(jnp.int32, (lanes, lanes), 0)
    left = []
    right = []
    for value, lane, block in items:
        high = value.astype(bf16).astype(f32)
        part = jnp.where(sub < 3, high, value - high)
        block = rows_of(block)
        left.append(
            jnp.concatenate(
                [jnp.where(block == number, part, 0.0) for number in range(block_count)], axis=0
            ).astype(bf16)
        )
        if marks is not None:
            continue
        right.append(
            jnp.where(spot == jnp.broadcast_to(lane, (lanes, lanes)), 1.0, 0.0).astype(bf16)
        )
    return lax.dot_general(
        jnp.concatenate(left, axis=1),
        jnp.concatenate(right, axis=1) if marks is None else marks,
        (((1,), (1,)), ((), ())),
        preferred_element_type=f32,
    )


def twice(value):
    return jnp.concatenate([value, value, value[:2]], axis=0)


def summed(product, number):
    return product[8 * number : 8 * number + 3] + product[8 * number + 3 : 8 * number + 6]


def start_kernel(disp, vel, force, trans_send, displaced_out, trans_out):
    displaced = disp[...] + drift_step * (vel[...] + kick_factor * force[...])
    displaced_out[...] = displaced
    width = trans_send.shape[1]
    blocks = [
        pad_rows(displaced[:, lanes * b : lanes * (b + 1)]) for b in range(displaced.shape[1] // lanes)
    ]
    for way in range(2):
        column = pad_lanes(trans_send[way : way + 1, :])
        trans_out[way] = pick_columns(blocks, column)[:3, :width]


def prepare_kernel(
    shock_send,
    neighbour_block,
    neighbour_lane,
    beta,
    alpha,
    trans_like,
    shock_spots_out,
    spots_out,
    linear_out,
    matrix_out,
):
    neighbours, slots = neighbour_block.shape
    halves = slots // lanes
    width = trans_like.shape[2]
    column = neighbour_block[...] * lanes + neighbour_lane[...]
    column = jnp.where(column >= slots + 2 * width, column + (lanes - 2 * width), column)
    even = lax.axis_index("shock") % 2 == 0
    border = (halves + 1) * lanes
    turned = column + lanes * (2 * halves + 3) - 2 * (column & -lanes)
    column = jnp.where(even & (column >= border), turned, column)
    column = jnp.where(neighbour_block[...] < 0, -1, column)
    spots_out[...] = jnp.full(spots_out.shape, -1, jnp.int32)
    for number in range(halves):
        spots_out[pl.ds(number, neighbours, stride=halves), :] = column[
            :, lanes * number : lanes * (number + 1)
        ]
    shock_spots_out[0:1, :] = jnp.where(even, shock_send[1:2, :], shock_send[0:1, :])
    shock_spots_out[1:2, :] = jnp.where(even, shock_send[0:1, :], shock_send[1:2, :])
    matrix = alpha[...]
    count = matrix.shape[0]
    matrix_out[...] = 0.5 * (matrix + matrix.T)
    eye = lax.broadcasted_iota(jnp.int32, (count, count), 0) == lax.broadcasted_iota(
        jnp.int32, (count, count), 1
    )
    linear = jnp.sum(
        jnp.where(eye, jnp.broadcast_to(beta[...], (count, count)), 0.0), axis=1, keepdims=True
    )
    linear_out[...] = jnp.broadcast_to(linear, linear_out.shape)


def settle_kernel(
    counts,
    vel,
    force,
    trans_send,
    leaving_slots,
    after,
    half_out,
    kept_out,
    trans_spots_out,
    leaving_out,
):
    slots = vel.shape[1]
    half_out[...] = vel[...] + kick_factor * force[...]
    trans_spots_out[...] = pad_lanes(trans_send[...], -1)
    leaving = leaving_slots.shape[1]
    entry = lax.broadcasted_iota(jnp.int32, (1, leaving), 1)
    going = jnp.where(entry < jnp.broadcast_to(counts[:, 1:2], (1, leaving)), leaving_slots[...], -1)
    leaving_out[...] = pad_lanes(going, -1)
    square = (leaving, leaving)
    eye = lax.broadcasted_iota(jnp.int32, square, 0) == lax.broadcasted_iota(jnp.int32, square, 1)
    upright = jnp.sum(
        jnp.where(eye, jnp.broadcast_to(going, square).astype(f32), 0.0), axis=1, keepdims=True
    )
    slot = lax.broadcasted_iota(jnp.int32, (leaving, slots), 1)
    gone = jnp.where(slot.astype(f32) == jnp.broadcast_to(upright, slot.shape), 1.0, 0.0)
    gone = jnp.sum(gone, axis=0, keepdims=True)
    live = slot[:1] < jnp.broadcast_to(counts[:, 0:1], (1, slots))
    kept_out[...] = jnp.where(live, 1.0 - gone, 0.0)


def mark_kernel(spots, marks_out):
    spot = lax.broadcasted_iota(jnp.int32, (lanes, lanes), 0)
    for row in range(marks_out.shape[1] // lanes):
        lane = jnp.broadcast_to(spots[row : row + 1, :] & (lanes - 1), (lanes, lanes))
        marks_out[:, lanes * row : lanes * (row + 1)] = jnp.where(spot == lane, 1.0, 0.0).astype(bf16)


def shock_kernel(displaced, trans_in, shock_spots, first_out, second_out, trans_block):
    width = trans_in.shape[2]
    trans_block[...] = jnp.zeros(trans_block.shape, f32)
    trans_block[:3, :width] = trans_in[1]
    trans_block[:3, width : 2 * width] = trans_in[0]
    blocks = [
        pad_rows(displaced[:, lanes * b : lanes * (b + 1)]) for b in range(displaced.shape[1] // lanes)
    ]
    blocks.append(trans_block[...])
    for way, out in enumerate((first_out, second_out)):
        out[...] = pick_columns(blocks, shock_spots[way : way + 1, :])[:3]


def energy_kernel(
    displaced,
    trans_in,
    from_first,
    from_second,
    spots,
    linear,
    matrix,
    marks,
    energy_out,
    own_out,
    trans_out,
    first_out,
    second_out,
    trans_block,
    grads,
    packed,
):
    slots = displaced.shape[1]
    width = trans_in.shape[2]
    halves = slots // lanes
    per_group = 8 // halves
    groups = spots.shape[0] // 8
    own_blocks = halves
    block_count = own_blocks + 3
    sub = lax.broadcasted_iota(jnp.int32, (8, lanes), 0)
    half_of = sub % halves
    which = sub // halves

    def by_half(pieces):
        out = rows_of(pieces[0])
        for number in range(1, halves):
            out = jnp.where(half_of == number, rows_of(pieces[number]), out)
        return out

    def by_which(values):
        out = jnp.full((8, lanes), values[0], f32)
        for number in range(1, per_group):
            if any(v != values[0] for v in values):
                out = jnp.where(which == number, values[number], out)
        return out

    def over_group(value):
        shift = 4
        while shift >= halves:
            value = value + pltpu.roll(value, shift, 0)
            shift //= 2
        return value

    trans_block[...] = jnp.zeros(trans_block.shape, f32)
    trans_block[:3, :width] = trans_in[1]
    trans_block[:3, width : 2 * width] = trans_in[0]

    def table(axis):
        pieces = [displaced[axis : axis + 1, lanes * b : lanes * (b + 1)] for b in range(own_blocks)]
        pieces.append(trans_block[axis : axis + 1, :])
        pieces.append(from_first[axis : axis + 1, :])
        pieces.append(from_second[axis : axis + 1, :])
        return pieces

    tables = [table(axis) for axis in range(3)]
    own = [by_half(tables[axis][:own_blocks]) for axis in range(3)]
    spread = [[rows_of(piece) for piece in tables[axis]] for axis in range(3)]
    offsets = lattice_list()
    neighbours = len(offsets)
    offsets = offsets + [offsets[0]] * (groups * per_group - neighbours)

    directions = []
    radials = []
    slopes = []
    inverses = []
    for group in range(groups):
        spot = spots[8 * group : 8 * group + 8, :]
        live = spot >= 0
        lane = jnp.where(live, spot & (lanes - 1), 0)
        block = jnp.where(live, spot >> 7, 0)
        vector = []
        for axis in range(3):
            picked = pick_lanes(spread[axis][0], lane)
            for number in range(1, block_count):
                picked = jnp.where(block == number, pick_lanes(spread[axis][number], lane), picked)
            offset = by_which([offsets[per_group * group + i][axis] for i in range(per_group)])
            vector.append(offset + picked - own[axis])
        square = vector[0] * vector[0] + vector[1] * vector[1] + vector[2] * vector[2]
        inverse = lax.rsqrt(square)
        distance = square * inverse
        directions.append([v * inverse for v in vector])
        inverses.append(inverse)
        angle = distance * (math.pi / cutoff_radius) - (math.pi / 2)
        squared = angle * angle
        sine = jnp.full_like(angle, -1.0 / math.factorial(15))
        for order in (13, 11, 9, 7, 5, 3, 1):
            sine = sine * squared + ((-1.0) ** ((order - 1) // 2)) / math.factorial(order)
        sine = sine * angle
        cosine = jnp.full_like(angle, 1.0 / math.factorial(16))
        for order in (14, 12, 10, 8, 6, 4, 2, 0):
            cosine = cosine * squared + ((-1.0) ** (order // 2)) / math.factorial(order)
        half = jnp.where(live, 0.5, 0.0)
        smooth = half - half * sine
        smooth_slope = half * cosine * (-math.pi / cutoff_radius)
        radial = []
        slope = []
        for center in radial_centers:
            away = (distance - center) * (1.0 / radial_width)
            bell = jnp.exp(-away * away)
            radial.append(smooth * bell)
            slope.append(bell * (smooth_slope - smooth * away * (2.0 / radial_width)))
        radials.append(radial)
        slopes.append(slope)

    scaled = [
        [
            [direction[axis] * (1.0 / power) if power > 1 else direction[axis] for power in range(1, degrees)]
            for axis in range(3)
        ]
        for direction in directions
    ]
    monomials = {}
    kinds = len(radial_centers)
    moments = {}
    for triple in exponents:
        p, q, w = triple
        if p + q + w == 0:
            monomials[triple] = None
        else:
            axis = 0 if p else (1 if q else 2)
            lower = tuple(v - (1 if a == axis else 0) for a, v in enumerate(triple))
            values = []
            for group in range(groups):
                factor = scaled[group][axis][triple[axis] - 1]
                before = monomials[lower]
                values.append(factor if before is None else before[group] * factor)
            monomials[triple] = values
        for kind in range(kinds):
            total = None
            for group in range(groups):
                term = radials[group][kind]
                if monomials[triple] is not None:
                    term = term * monomials[triple][group]
                total = term if total is None else total + term
            moments[kind, triple] = over_group(total)

    weighted = {}
    for triple in exponents:
        weight = moment_scale**2 * math.factorial(sum(triple))
        for power in triple:
            weight *= math.factorial(power)
        for kind in range(kinds):
            weighted[kind, triple] = moments[kind, triple] * weight
    descriptor = []
    for first, second in pair_list:
        for degree in range(degrees):
            total = None
            for triple in exponents:
                if sum(triple) == degree:
                    term = weighted[first, triple] * moments[second, triple]
                    total = term if total is None else total + term
            descriptor.append(total)
    count = len(descriptor)
    padded = packed.shape[1] // 8 * per_group
    for start in range(0, padded, per_group):
        out = descriptor[min(start, count - 1)]
        for number in range(1, per_group):
            out = jnp.where(which == number, descriptor[min(start + number, count - 1)], out)
        packed[0, start * halves : start * halves + 8, :] = out
    features = jnp.concatenate(
        [packed[0, pl.ds(number, count, stride=halves), :] for number in range(halves)], axis=1
    )
    slope = linear[...] + lax.dot_general(
        matrix[...], features, (((1,), (0,)), ((), ())), precision=highest, preferred_element_type=f32
    )
    energy_out[...] = 0.5 * jnp.sum(features * (linear[...] + slope), axis=0, keepdims=True)
    for number in range(halves):
        packed[1, pl.ds(number, count, stride=halves), :] = slope[:, lanes * number : lanes * (number + 1)]

    sensitivities = []
    for number in range(count):
        sensitivities.append(
            by_half([packed[1, number * halves + h : number * halves + h + 1, :] for h in range(halves)])
        )
    backs = {}
    for triple in exponents:
        degree = sum(triple)
        for kind in range(kinds):
            total = None
            for place, (first, second) in enumerate(pair_list):
                if kind not in (first, second):
                    continue
                other = second if kind == first else first
                term = sensitivities[place * degrees + degree]
                if first == second:
                    term = term + term
                term = term * weighted[other, triple]
                total = term if total is None else total + term
            backs[kind, triple] = total

    sums = [None] * 3
    for group in range(groups):
        along = None
        tangent = [None] * 3
        for triple in exponents:
            mono = None if sum(triple) == 0 else monomials[triple][group]
            weight = None
            rise = None
            for kind in range(kinds):
                back = backs[kind, triple]
                term = slopes[group][kind] * back
                rise = term if rise is None else rise + term
                if mono is not None:
                    term = radials[group][kind] * back
                    weight = term if weight is None else weight + term
            if mono is not None:
                rise = rise * mono
            along = rise if along is None else along + rise
            if mono is None:
                continue
            for axis in range(3):
                if triple[axis] == 0:
                    continue
                lower = tuple(v - (1 if a == axis else 0) for a, v in enumerate(triple))
                term = weight if monomials[lower] is None else weight * monomials[lower][group]
                tangent[axis] = term if tangent[axis] is None else tangent[axis] + term
        direction = directions[group]
        radial_part = (
            direction[0] * tangent[0] + direction[1] * tangent[1] + direction[2] * tangent[2]
        )
        straight = along - radial_part * inverses[group]
        for axis in range(3):
            gradient = direction[axis] * straight + tangent[axis] * inverses[group]
            grads[axis, 8 * group : 8 * group + 8, :] = gradient
            sums[axis] = gradient if sums[axis] is None else sums[axis] + gradient

    items = []
    for row in range(neighbours * halves):
        value = jnp.where(
            (sub == 0) | (sub == 3),
            rows_of(grads[0, row : row + 1, :]),
            jnp.where(
                (sub == 1) | (sub == 4),
                rows_of(grads[1, row : row + 1, :]),
                rows_of(grads[2, row : row + 1, :]),
            ),
        )
        spot = spots[row : row + 1, :]
        items.append((value, spot & (lanes - 1), spot >> 7))
    product = scatter_product(items, block_count, marks[...])
    totals = [over_group(value) for value in sums]
    for number in range(own_blocks):
        self_part = jnp.concatenate([totals[axis][number : number + 1] for axis in range(3)], axis=0)
        own_out[:, lanes * number : lanes * (number + 1)] = summed(product, number) - self_part
    trans_out[...] = summed(product, own_blocks)
    first_out[...] = summed(product, own_blocks + 1)
    second_out[...] = summed(product, own_blocks + 2)


def shock_back_kernel(own, trans, back_first, back_second, shock_spots, own_out, trans_out):
    own_blocks = own.shape[1] // lanes
    width = trans_out.shape[2]
    items = []
    for way, back in enumerate((back_first, back_second)):
        spot = shock_spots[way : way + 1, :]
        items.append((twice(back[...]), spot & (lanes - 1), spot >> 7))
    product = scatter_product(items, own_blocks + 1)
    for number in range(own_blocks):
        cut = slice(lanes * number, lanes * (number + 1))
        own_out[:, cut] = own[:, cut] + summed(product, number)
    ghosts = trans[...] + summed(product, own_blocks)
    trans_out[0] = ghosts[:, :width]
    trans_out[1] = ghosts[:, width : 2 * width]


def force_kernel(half_velocity, displaced, own, back, trans_spots, leaving_spots, force_out, payload_out):
    own_blocks = own.shape[1] // lanes
    items = []
    for way in range(2):
        spot = trans_spots[way : way + 1, :]
        items.append((twice(pad_lanes(back[1 - way])), spot & (lanes - 1), spot >> 7))
    product = scatter_product(items, own_blocks)
    leaving = payload_out.shape[2]
    blocks = []
    for number in range(own_blocks):
        cut = slice(lanes * number, lanes * (number + 1))
        new_force = -(own[:, cut] + summed(product, number))
        force_out[:, cut] = new_force
        new_velocity = half_velocity[:, cut] + kick_factor * new_force
        blocks.append(
            jnp.concatenate(
                [pad_rows(displaced[:, cut]), pad_rows(new_velocity), pad_rows(new_force)], axis=0
            )
        )
    picked = pick_columns(blocks, leaving_spots[...])
    for number in range(3):
        payload_out[number] = picked[8 * number : 8 * number + 3, :leaving]


def write_kernel(half_velocity, kept, displaced, new_force, energy, disp_out, vel_out, force_out, energy_out):
    keep = kept[...]
    force = new_force[...]
    disp_out[...] = displaced[...] * keep
    vel_out[...] = (half_velocity[...] + kick_factor * force) * keep
    force_out[...] = force * keep
    energy_out[...] = energy[...] * keep


def along_shock(x, by):
    devices = lax.axis_size("shock")
    return lax.ppermute(
        x, "shock", [(i, i + by) for i in range(devices) if 0 <= i + by < devices]
    )


def with_partner(x, start):
    devices = lax.axis_size("shock")
    lows = range(start, devices - 1, 2)
    return lax.ppermute(x, "shock", [(i, i + 1) for i in lows] + [(i + 1, i) for i in lows])


def across(x):
    devices = lax.axis_size("trans")
    down = [(i, (i - 1) % devices) for i in range(devices)]
    up = [(i, (i + 1) % devices) for i in range(devices)]
    if sorted(down) == sorted(up):
        return lax.ppermute(x, "trans", down)
    return jnp.stack([lax.ppermute(x[0], "trans", down), lax.ppermute(x[1], "trans", up)])


def shaped(*dims, kind=f32):
    return pltpu.VMEM(dims, kind)


def run_kernel(kernel, out_shape, args, scratch=(), far=0, cost=None):
    vmem = pl.BlockSpec(memory_space=pltpu.VMEM)
    args = [
        arg if place < far else pltpu.with_memory_space_constraint(arg, pltpu.VMEM)
        for place, arg in enumerate(args)
    ]
    return pl.pallas_call(
        kernel,
        in_specs=[vmem] * len(args),
        out_specs=tuple(vmem for _ in out_shape),
        out_shape=out_shape,
        scratch_shapes=list(scratch),
        cost_estimate=cost,
    )(*args)


def shards(
    displacement,
    velocity,
    force_before,
    beta,
    alpha,
    live_count,
    trans_send,
    shock_send,
    neighbour_block,
    neighbour_lane,
    leaving_slots,
    leaving_count,
):
    slots = displacement.shape[1]
    trans_width = trans_send.shape[1]
    shock_width = shock_send.shape[1]
    neighbours = neighbour_block.shape[0]
    leaving = leaving_slots.shape[0]
    halves = slots // lanes
    groups = -(-neighbours // (8 // halves))
    count = len(pair_list) * degrees
    assert slots % lanes == 0 and 8 % halves == 0 and halves <= 4
    assert shock_width == lanes and 2 * trans_width <= lanes
    displaced, trans_go = run_kernel(
        start_kernel,
        (shaped(3, slots), shaped(2, 3, trans_width)),
        (displacement, velocity, force_before, trans_send),
        far=4,
    )
    trans_in = across(trans_go)
    whole = jnp.int32
    shock_spots, spots, linear, matrix = run_kernel(
        prepare_kernel,
        (
            shaped(2, shock_width, kind=whole),
            shaped(groups * 8, lanes, kind=whole),
            shaped(count, slots),
            shaped(count, count),
        ),
        (shock_send, neighbour_block, neighbour_lane, beta.reshape(1, count), alpha, trans_go),
        far=5,
        cost=pl.CostEstimate(flops=40 * slots * neighbours, bytes_accessed=12 * slots * neighbours, transcendentals=0),
    )
    to_first, to_second = run_kernel(
        shock_kernel,
        (shaped(3, shock_width), shaped(3, shock_width)),
        (displaced, trans_in, shock_spots),
        (pltpu.VMEM((8, lanes), f32),),
    )
    from_second = with_partner(to_second, 1)
    from_first = with_partner(to_first, 0)
    (marks,) = run_kernel(
        mark_kernel,
        (shaped(lanes, neighbours * slots, kind=bf16),),
        (spots,),
        cost=pl.CostEstimate(
            flops=2 * lanes * neighbours * slots, bytes_accessed=2 * lanes * neighbours * slots, transcendentals=0
        ),
    )
    packed_rows = -(-(count * halves) // 8) * 8
    energy, own, trans, first, second = run_kernel(
        energy_kernel,
        (shaped(1, slots), shaped(3, slots), shaped(3, lanes), shaped(3, lanes), shaped(3, lanes)),
        (displaced, trans_in, from_first, from_second, spots, linear, matrix, marks),
        (
            pltpu.VMEM((8, lanes), f32),
            pltpu.VMEM((3, groups * 8, lanes), f32),
            pltpu.VMEM((2, packed_rows, lanes), f32),
        ),
    )
    back_second = with_partner(second, 1)
    back_first = with_partner(first, 0)
    half_velocity, kept, trans_spots, leaving_spots = run_kernel(
        settle_kernel,
        (
            shaped(3, slots),
            shaped(1, slots),
            shaped(2, lanes, kind=whole),
            shaped(1, lanes, kind=whole),
        ),
        (
            jnp.concatenate([live_count, leaving_count]).reshape(1, 2),
            velocity,
            force_before,
            trans_send,
            leaving_slots.reshape(1, leaving),
            own,
        ),
        far=5,
        cost=pl.CostEstimate(flops=40 * slots, bytes_accessed=400 * slots, transcendentals=0),
    )
    own, trans_go = run_kernel(
        shock_back_kernel,
        (shaped(3, slots), shaped(2, 3, trans_width)),
        (own, trans, back_first, back_second, shock_spots),
    )
    back = across(trans_go)
    new_force, payload = run_kernel(
        force_kernel,
        (shaped(3, slots), shaped(3, 3, leaving)),
        (half_velocity, displaced, own, back, trans_spots, leaving_spots),
    )
    wide = jax.ShapeDtypeStruct((3, slots), f32)
    disp_next, vel_next, force_next, energy = run_kernel(
        write_kernel,
        (wide, wide, wide, jax.ShapeDtypeStruct((1, slots), f32)),
        (half_velocity, kept, displaced, new_force, energy),
        cost=pl.CostEstimate(flops=9 * slots, bytes_accessed=80 * slots, transcendentals=0),
    )
    arrivals = along_shock(payload, -1)
    return (disp_next, vel_next, force_next, energy.reshape(slots), arrivals)


def solution(mesh):
    both = ("shock", "trans")
    in_specs = (
        P(None, both),
        P(None, both),
        P(None, both),
        P(),
        P(),
        P(both),
        P(None, both),
        P(None, both),
        P(None, both),
        P(None, both),
        P(both),
        P(both),
    )
    out_specs = (P(None, both), P(None, both), P(None, both), P(both), P(None, None, both))
    return jax.shard_map(shards, mesh=mesh, in_specs=in_specs, out_specs=out_specs, check_vma=False)
```

```python
import math

import jax
import jax.numpy as jnp
from jax import lax
from jax.experimental import pallas as pl
from jax.experimental.pallas import tpu as pltpu
from jax.sharding import PartitionSpec as P


kick_factor = 0.5
drift_step = 0.02
cutoff_radius = 4.2
radial_width = 0.35
radial_centers = (1.4, 1.9, 2.4, 2.9)
moment_scale = 0.25
pair_list = ((0, 0), (0, 1), (0, 2), (0, 3), (1, 1), (1, 2), (1, 3), (2, 2), (2, 3), (3, 3))
degrees = 5
lanes = 128
highest = lax.Precision.HIGHEST
f32 = jnp.float32
bf16 = jnp.bfloat16


def lattice_list():
    entries = []
    for number in range(8):
        entries.append(
            (1.0 - 2.0 * (number >> 2 & 1), 1.0 - 2.0 * (number >> 1 & 1), 1.0 - 2.0 * (number & 1))
        )
    for axis_pick in range(3):
        for signed in (2.0, -2.0):
            vector = [0.0, 0.0, 0.0]
            vector[axis_pick] = signed
            entries.append(tuple(vector))
    for zero_pick in (2, 1, 0):
        others = [axis_pick for axis_pick in range(3) if axis_pick != zero_pick]
        for leading in (2.0, -2.0):
            for trailing in (2.0, -2.0):
                vector = [0.0, 0.0, 0.0]
                vector[others[0]] = leading
                vector[others[1]] = trailing
                entries.append(tuple(vector))
    return entries


def exponent_list():
    return [
        (p, q, degree - p - q)
        for degree in range(degrees)
        for p in range(degree, -1, -1)
        for q in range(degree - p, -1, -1)
    ]


exponents = exponent_list()


def rows_of(value, count=8):
    return jnp.broadcast_to(value, (count,) + value.shape[1:])


def pick_lanes(table, index):
    return jnp.take_along_axis(table, index, axis=1, mode="promise_in_bounds")


def pick_columns(blocks, column):
    rows = blocks[0].shape[0]
    lane = rows_of(column & (lanes - 1), rows)
    block = rows_of(column >> 7, rows)
    out = jnp.zeros((rows, lanes), f32)
    for number, table in enumerate(blocks):
        out = jnp.where(block == number, pick_lanes(table, lane), out)
    return out


def pad_lanes(value, fill=0):
    rows, width = value.shape
    if width == lanes:
        return value
    return jnp.concatenate([value, jnp.full((rows, lanes - width), fill, value.dtype)], axis=1)


def pad_rows(value, count=8):
    rows = value.shape[0]
    return jnp.concatenate([value, jnp.zeros((count - rows,) + value.shape[1:], value.dtype)], axis=0)


def scatter_product(items, block_count, marks=None):
    sub = lax.broadcasted_iota(jnp.int32, (8, lanes), 0)
    spot = lax.broadcasted_iota(jnp.int32, (lanes, lanes), 0)
    left = []
    right = []
    for value, lane, block in items:
        high = value.astype(bf16).astype(f32)
        part = jnp.where(sub < 3, high, value - high)
        block = rows_of(block)
        left.append(
            jnp.concatenate(
                [jnp.where(block == number, part, 0.0) for number in range(block_count)], axis=0
            ).astype(bf16)
        )
        if marks is not None:
            continue
        right.append(
            jnp.where(spot == jnp.broadcast_to(lane, (lanes, lanes)), 1.0, 0.0).astype(bf16)
        )
    return lax.dot_general(
        jnp.concatenate(left, axis=1),
        jnp.concatenate(right, axis=1) if marks is None else marks,
        (((1,), (1,)), ((), ())),
        preferred_element_type=f32,
    )


def twice(value):
    return jnp.concatenate([value, value, value[:2]], axis=0)


def summed(product, number):
    return product[8 * number : 8 * number + 3] + product[8 * number + 3 : 8 * number + 6]


def start_kernel(disp, vel, force, trans_send, displaced_out, trans_out):
    displaced = disp[...] + drift_step * (vel[...] + kick_factor * force[...])
    displaced_out[...] = displaced
    width = trans_send.shape[1]
    blocks = [
        pad_rows(displaced[:, lanes * b : lanes * (b + 1)]) for b in range(displaced.shape[1] // lanes)
    ]
    for way in range(2):
        column = pad_lanes(trans_send[way : way + 1, :])
        trans_out[way] = pick_columns(blocks, column)[:3, :width]


def prepare_kernel(
    shock_send,
    neighbour_block,
    neighbour_lane,
    beta,
    alpha,
    trans_like,
    shock_spots_out,
    spots_out,
    linear_out,
    matrix_out,
):
    neighbours, slots = neighbour_block.shape
    halves = slots // lanes
    width = trans_like.shape[2]
    column = neighbour_block[...] * lanes + neighbour_lane[...]
    column = jnp.where(column >= slots + 2 * width, column + (lanes - 2 * width), column)
    even = lax.axis_index("shock") % 2 == 0
    border = (halves + 1) * lanes
    turned = column + lanes * (2 * halves + 3) - 2 * (column & -lanes)
    column = jnp.where(even & (column >= border), turned, column)
    column = jnp.where(neighbour_block[...] < 0, -1, column)
    spots_out[...] = jnp.full(spots_out.shape, -1, jnp.int32)
    for number in range(halves):
        spots_out[pl.ds(number, neighbours, stride=halves), :] = column[
            :, lanes * number : lanes * (number + 1)
        ]
    shock_spots_out[0:1, :] = jnp.where(even, shock_send[1:2, :], shock_send[0:1, :])
    shock_spots_out[1:2, :] = jnp.where(even, shock_send[0:1, :], shock_send[1:2, :])
    matrix = alpha[...]
    count = matrix.shape[0]
    matrix_out[...] = 0.5 * (matrix + matrix.T)
    eye = lax.broadcasted_iota(jnp.int32, (count, count), 0) == lax.broadcasted_iota(
        jnp.int32, (count, count), 1
    )
    linear = jnp.sum(
        jnp.where(eye, jnp.broadcast_to(beta[...], (count, count)), 0.0), axis=1, keepdims=True
    )
    linear_out[...] = jnp.broadcast_to(linear, linear_out.shape)


def settle_kernel(
    vel,
    force,
    trans_send,
    leaving_slots,
    count_row,
    after,
    half_out,
    stay_out,
    trans_spots_out,
    leaving_out,
):
    slots = vel.shape[1]
    half_out[...] = vel[...] + kick_factor * force[...]
    trans_spots_out[...] = pad_lanes(trans_send[...], -1)
    leaving = leaving_slots.shape[1]
    entry = lax.broadcasted_iota(jnp.int32, (1, leaving), 1)
    going = jnp.where(entry < count_row[:, :leaving], leaving_slots[...], -1)
    leaving_out[...] = pad_lanes(going, -1)
    square = (leaving, leaving)
    eye = lax.broadcasted_iota(jnp.int32, square, 0) == lax.broadcasted_iota(jnp.int32, square, 1)
    upright = jnp.sum(
        jnp.where(eye, jnp.broadcast_to(going, square).astype(f32), 0.0), axis=1, keepdims=True
    )
    slot = lax.broadcasted_iota(jnp.int32, (leaving, slots), 1)
    gone = jnp.where(slot.astype(f32) == jnp.broadcast_to(upright, slot.shape), 1.0, 0.0)
    gone = jnp.sum(gone, axis=0, keepdims=True)
    stay_out[...] = 1.0 - gone


def tally_kernel(leaving_count, count_out):
    count_out[...] = jnp.broadcast_to(leaving_count[...].reshape(1, 1), (1, lanes))


def mark_kernel(spots, marks_out):
    spot = lax.broadcasted_iota(jnp.int32, (lanes, lanes), 0)
    for row in range(marks_out.shape[1] // lanes):
        lane = jnp.broadcast_to(spots[row : row + 1, :] & (lanes - 1), (lanes, lanes))
        marks_out[:, lanes * row : lanes * (row + 1)] = jnp.where(spot == lane, 1.0, 0.0).astype(bf16)


def shock_kernel(displaced, trans_in, shock_spots, first_out, second_out, trans_block):
    width = trans_in.shape[2]
    trans_block[...] = jnp.zeros(trans_block.shape, f32)
    trans_block[:3, :width] = trans_in[1]
    trans_block[:3, width : 2 * width] = trans_in[0]
    blocks = [
        pad_rows(displaced[:, lanes * b : lanes * (b + 1)]) for b in range(displaced.shape[1] // lanes)
    ]
    blocks.append(trans_block[...])
    for way, out in enumerate((first_out, second_out)):
        out[...] = pick_columns(blocks, shock_spots[way : way + 1, :])[:3]


def energy_kernel(
    displaced,
    trans_in,
    from_first,
    from_second,
    spots,
    linear,
    matrix,
    marks,
    energy_out,
    own_out,
    trans_out,
    first_out,
    second_out,
    trans_block,
    grads,
    packed,
):
    slots = displaced.shape[1]
    width = trans_in.shape[2]
    halves = slots // lanes
    per_group = 8 // halves
    groups = spots.shape[0] // 8
    own_blocks = halves
    block_count = own_blocks + 3
    sub = lax.broadcasted_iota(jnp.int32, (8, lanes), 0)
    half_of = sub % halves
    which = sub // halves

    def by_half(pieces):
        out = rows_of(pieces[0])
        for number in range(1, halves):
            out = jnp.where(half_of == number, rows_of(pieces[number]), out)
        return out

    def by_which(values):
        out = jnp.full((8, lanes), values[0], f32)
        for number in range(1, per_group):
            if any(v != values[0] for v in values):
                out = jnp.where(which == number, values[number], out)
        return out

    def over_group(value):
        shift = 4
        while shift >= halves:
            value = value + pltpu.roll(value, shift, 0)
            shift //= 2
        return value

    trans_block[...] = jnp.zeros(trans_block.shape, f32)
    trans_block[:3, :width] = trans_in[1]
    trans_block[:3, width : 2 * width] = trans_in[0]

    def table(axis):
        pieces = [displaced[axis : axis + 1, lanes * b : lanes * (b + 1)] for b in range(own_blocks)]
        pieces.append(trans_block[axis : axis + 1, :])
        pieces.append(from_first[axis : axis + 1, :])
        pieces.append(from_second[axis : axis + 1, :])
        return pieces

    tables = [table(axis) for axis in range(3)]
    own = [by_half(tables[axis][:own_blocks]) for axis in range(3)]
    spread = [[rows_of(piece) for piece in tables[axis]] for axis in range(3)]
    offsets = lattice_list()
    neighbours = len(offsets)
    offsets = offsets + [offsets[0]] * (groups * per_group - neighbours)

    directions = []
    radials = []
    slopes = []
    inverses = []
    for group in range(groups):
        spot = spots[8 * group : 8 * group + 8, :]
        live = spot >= 0
        lane = jnp.where(live, spot & (lanes - 1), 0)
        block = jnp.where(live, spot >> 7, 0)
        vector = []
        for axis in range(3):
            picked = pick_lanes(spread[axis][0], lane)
            for number in range(1, block_count):
                picked = jnp.where(block == number, pick_lanes(spread[axis][number], lane), picked)
            offset = by_which([offsets[per_group * group + i][axis] for i in range(per_group)])
            vector.append(offset + picked - own[axis])
        square = vector[0] * vector[0] + vector[1] * vector[1] + vector[2] * vector[2]
        inverse = lax.rsqrt(square)
        distance = square * inverse
        directions.append([v * inverse for v in vector])
        inverses.append(inverse)
        angle = distance * (math.pi / cutoff_radius) - (math.pi / 2)
        squared = angle * angle
        sine = jnp.full_like(angle, -1.0 / math.factorial(15))
        for order in (13, 11, 9, 7, 5, 3, 1):
            sine = sine * squared + ((-1.0) ** ((order - 1) // 2)) / math.factorial(order)
        sine = sine * angle
        cosine = jnp.full_like(angle, 1.0 / math.factorial(16))
        for order in (14, 12, 10, 8, 6, 4, 2, 0):
            cosine = cosine * squared + ((-1.0) ** (order // 2)) / math.factorial(order)
        half = jnp.where(live, 0.5, 0.0)
        smooth = half - half * sine
        smooth_slope = half * cosine * (-math.pi / cutoff_radius)
        radial = []
        slope = []
        for center in radial_centers:
            away = (distance - center) * (1.0 / radial_width)
            bell = jnp.exp(-away * away)
            radial.append(smooth * bell)
            slope.append(bell * (smooth_slope - smooth * away * (2.0 / radial_width)))
        radials.append(radial)
        slopes.append(slope)

    scaled = [
        [
            [direction[axis] * (1.0 / power) if power > 1 else direction[axis] for power in range(1, degrees)]
            for axis in range(3)
        ]
        for direction in directions
    ]
    monomials = {}
    kinds = len(radial_centers)
    moments = {}
    for triple in exponents:
        p, q, w = triple
        if p + q + w == 0:
            monomials[triple] = None
        else:
            axis = 0 if p else (1 if q else 2)
            lower = tuple(v - (1 if a == axis else 0) for a, v in enumerate(triple))
            values = []
            for group in range(groups):
                factor = scaled[group][axis][triple[axis] - 1]
                before = monomials[lower]
                values.append(factor if before is None else before[group] * factor)
            monomials[triple] = values
        for kind in range(kinds):
            total = None
            for group in range(groups):
                term = radials[group][kind]
                if monomials[triple] is not None:
                    term = term * monomials[triple][group]
                total = term if total is None else total + term
            moments[kind, triple] = over_group(total)

    weighted = {}
    for triple in exponents:
        weight = moment_scale**2 * math.factorial(sum(triple))
        for power in triple:
            weight *= math.factorial(power)
        for kind in range(kinds):
            weighted[kind, triple] = moments[kind, triple] * weight
    descriptor = []
    for first, second in pair_list:
        for degree in range(degrees):
            total = None
            for triple in exponents:
                if sum(triple) == degree:
                    term = weighted[first, triple] * moments[second, triple]
                    total = term if total is None else total + term
            descriptor.append(total)
    count = len(descriptor)
    padded = packed.shape[1] // 8 * per_group
    for start in range(0, padded, per_group):
        out = descriptor[min(start, count - 1)]
        for number in range(1, per_group):
            out = jnp.where(which == number, descriptor[min(start + number, count - 1)], out)
        packed[0, start * halves : start * halves + 8, :] = out
    features = jnp.concatenate(
        [packed[0, pl.ds(number, count, stride=halves), :] for number in range(halves)], axis=1
    )
    slope = linear[...] + lax.dot_general(
        matrix[...], features, (((1,), (0,)), ((), ())), precision=highest, preferred_element_type=f32
    )
    energy_out[...] = 0.5 * jnp.sum(features * (linear[...] + slope), axis=0, keepdims=True)
    for number in range(halves):
        packed[1, pl.ds(number, count, stride=halves), :] = slope[:, lanes * number : lanes * (number + 1)]

    sensitivities = []
    for number in range(count):
        sensitivities.append(
            by_half([packed[1, number * halves + h : number * halves + h + 1, :] for h in range(halves)])
        )
    backs = {}
    for triple in exponents:
        degree = sum(triple)
        for kind in range(kinds):
            total = None
            for place, (first, second) in enumerate(pair_list):
                if kind not in (first, second):
                    continue
                other = second if kind == first else first
                term = sensitivities[place * degrees + degree]
                if first == second:
                    term = term + term
                term = term * weighted[other, triple]
                total = term if total is None else total + term
            backs[kind, triple] = total

    sums = [None] * 3
    for group in range(groups):
        along = None
        tangent = [None] * 3
        for triple in exponents:
            mono = None if sum(triple) == 0 else monomials[triple][group]
            weight = None
            rise = None
            for kind in range(kinds):
                back = backs[kind, triple]
                term = slopes[group][kind] * back
                rise = term if rise is None else rise + term
                if mono is not None:
                    term = radials[group][kind] * back
                    weight = term if weight is None else weight + term
            if mono is not None:
                rise = rise * mono
            along = rise if along is None else along + rise
            if mono is None:
                continue
            for axis in range(3):
                if triple[axis] == 0:
                    continue
                lower = tuple(v - (1 if a == axis else 0) for a, v in enumerate(triple))
                term = weight if monomials[lower] is None else weight * monomials[lower][group]
                tangent[axis] = term if tangent[axis] is None else tangent[axis] + term
        direction = directions[group]
        radial_part = (
            direction[0] * tangent[0] + direction[1] * tangent[1] + direction[2] * tangent[2]
        )
        straight = along - radial_part * inverses[group]
        for axis in range(3):
            gradient = direction[axis] * straight + tangent[axis] * inverses[group]
            grads[axis, 8 * group : 8 * group + 8, :] = gradient
            sums[axis] = gradient if sums[axis] is None else sums[axis] + gradient

    items = []
    for row in range(neighbours * halves):
        value = jnp.where(
            (sub == 0) | (sub == 3),
            rows_of(grads[0, row : row + 1, :]),
            jnp.where(
                (sub == 1) | (sub == 4),
                rows_of(grads[1, row : row + 1, :]),
                rows_of(grads[2, row : row + 1, :]),
            ),
        )
        spot = spots[row : row + 1, :]
        items.append((value, spot & (lanes - 1), spot >> 7))
    product = scatter_product(items, block_count, marks[...])
    totals = [over_group(value) for value in sums]
    for number in range(own_blocks):
        self_part = jnp.concatenate([totals[axis][number : number + 1] for axis in range(3)], axis=0)
        own_out[:, lanes * number : lanes * (number + 1)] = summed(product, number) - self_part
    trans_out[...] = summed(product, own_blocks)
    first_out[...] = summed(product, own_blocks + 1)
    second_out[...] = summed(product, own_blocks + 2)


def shock_back_kernel(own, trans, back_first, back_second, shock_spots, own_out, trans_out):
    own_blocks = own.shape[1] // lanes
    width = trans_out.shape[2]
    items = []
    for way, back in enumerate((back_first, back_second)):
        spot = shock_spots[way : way + 1, :]
        items.append((twice(back[...]), spot & (lanes - 1), spot >> 7))
    product = scatter_product(items, own_blocks + 1)
    for number in range(own_blocks):
        cut = slice(lanes * number, lanes * (number + 1))
        own_out[:, cut] = own[:, cut] + summed(product, number)
    ghosts = trans[...] + summed(product, own_blocks)
    trans_out[0] = ghosts[:, :width]
    trans_out[1] = ghosts[:, width : 2 * width]


def force_kernel(half_velocity, displaced, own, back, trans_spots, leaving_spots, force_out, payload_out):
    own_blocks = own.shape[1] // lanes
    items = []
    for way in range(2):
        spot = trans_spots[way : way + 1, :]
        items.append((twice(pad_lanes(back[1 - way])), spot & (lanes - 1), spot >> 7))
    product = scatter_product(items, own_blocks)
    leaving = payload_out.shape[2]
    blocks = []
    for number in range(own_blocks):
        cut = slice(lanes * number, lanes * (number + 1))
        new_force = -(own[:, cut] + summed(product, number))
        force_out[:, cut] = new_force
        new_velocity = half_velocity[:, cut] + kick_factor * new_force
        blocks.append(
            jnp.concatenate(
                [pad_rows(displaced[:, cut]), pad_rows(new_velocity), pad_rows(new_force)], axis=0
            )
        )
    picked = pick_columns(blocks, leaving_spots[...])
    for number in range(3):
        payload_out[number] = picked[8 * number : 8 * number + 3, :leaving]


def write_kernel(
    live_count, half_velocity, stay, displaced, new_force, energy, disp_out, vel_out, force_out, energy_out
):
    slot = lax.broadcasted_iota(jnp.int32, stay.shape, 1)
    live = slot < jnp.broadcast_to(live_count[...].reshape(1, 1), stay.shape)
    keep = jnp.where(live, stay[...], 0.0)
    force = new_force[...]
    disp_out[...] = displaced[...] * keep
    vel_out[...] = (half_velocity[...] + kick_factor * force) * keep
    force_out[...] = force * keep
    energy_out[...] = energy[...] * keep


def along_shock(x, by):
    devices = lax.axis_size("shock")
    return lax.ppermute(
        x, "shock", [(i, i + by) for i in range(devices) if 0 <= i + by < devices]
    )


def with_partner(x, start):
    devices = lax.axis_size("shock")
    lows = range(start, devices - 1, 2)
    return lax.ppermute(x, "shock", [(i, i + 1) for i in lows] + [(i + 1, i) for i in lows])


def across(x):
    devices = lax.axis_size("trans")
    down = [(i, (i - 1) % devices) for i in range(devices)]
    up = [(i, (i + 1) % devices) for i in range(devices)]
    if sorted(down) == sorted(up):
        return lax.ppermute(x, "trans", down)
    return jnp.stack([lax.ppermute(x[0], "trans", down), lax.ppermute(x[1], "trans", up)])


def shaped(*dims, kind=f32):
    return pltpu.VMEM(dims, kind)


def run_kernel(kernel, out_shape, args, scratch=(), far=0, cost=None):
    vmem = pl.BlockSpec(memory_space=pltpu.VMEM)
    args = [
        arg if place < far else pltpu.with_memory_space_constraint(arg, pltpu.VMEM)
        for place, arg in enumerate(args)
    ]
    return pl.pallas_call(
        kernel,
        in_specs=[vmem] * len(args),
        out_specs=tuple(vmem for _ in out_shape),
        out_shape=out_shape,
        scratch_shapes=list(scratch),
        cost_estimate=cost,
    )(*args)


def shards(
    displacement,
    velocity,
    force_before,
    beta,
    alpha,
    live_count,
    trans_send,
    shock_send,
    neighbour_block,
    neighbour_lane,
    leaving_slots,
    leaving_count,
):
    slots = displacement.shape[1]
    trans_width = trans_send.shape[1]
    shock_width = shock_send.shape[1]
    neighbours = neighbour_block.shape[0]
    leaving = leaving_slots.shape[0]
    halves = slots // lanes
    groups = -(-neighbours // (8 // halves))
    count = len(pair_list) * degrees
    assert slots % lanes == 0 and 8 % halves == 0 and halves <= 4
    assert shock_width == lanes and 2 * trans_width <= lanes
    displaced, trans_go = run_kernel(
        start_kernel,
        (shaped(3, slots), shaped(2, 3, trans_width)),
        (displacement, velocity, force_before, trans_send),
        far=4,
    )
    trans_in = across(trans_go)
    whole = jnp.int32
    shock_spots, spots, linear, matrix = run_kernel(
        prepare_kernel,
        (
            shaped(2, shock_width, kind=whole),
            shaped(groups * 8, lanes, kind=whole),
            shaped(count, slots),
            shaped(count, count),
        ),
        (shock_send, neighbour_block, neighbour_lane, beta.reshape(1, count), alpha, trans_go),
        far=5,
        cost=pl.CostEstimate(flops=40 * slots * neighbours, bytes_accessed=12 * slots * neighbours, transcendentals=0),
    )
    to_first, to_second = run_kernel(
        shock_kernel,
        (shaped(3, shock_width), shaped(3, shock_width)),
        (displaced, trans_in, shock_spots),
        (pltpu.VMEM((8, lanes), f32),),
    )
    from_second = with_partner(to_second, 1)
    from_first = with_partner(to_first, 0)
    (count_row,) = run_kernel(tally_kernel, (shaped(1, lanes, kind=whole),), (leaving_count,), far=1)
    (marks,) = run_kernel(
        mark_kernel,
        (shaped(lanes, neighbours * slots, kind=bf16),),
        (spots,),
        cost=pl.CostEstimate(
            flops=2 * lanes * neighbours * slots, bytes_accessed=2 * lanes * neighbours * slots, transcendentals=0
        ),
    )
    packed_rows = -(-(count * halves) // 8) * 8
    energy, own, trans, first, second = run_kernel(
        energy_kernel,
        (shaped(1, slots), shaped(3, slots), shaped(3, lanes), shaped(3, lanes), shaped(3, lanes)),
        (displaced, trans_in, from_first, from_second, spots, linear, matrix, marks),
        (
            pltpu.VMEM((8, lanes), f32),
            pltpu.VMEM((3, groups * 8, lanes), f32),
            pltpu.VMEM((2, packed_rows, lanes), f32),
        ),
    )
    back_second = with_partner(second, 1)
    back_first = with_partner(first, 0)
    half_velocity, stay, trans_spots, leaving_spots = run_kernel(
        settle_kernel,
        (
            shaped(3, slots),
            shaped(1, slots),
            shaped(2, lanes, kind=whole),
            shaped(1, lanes, kind=whole),
        ),
        (
            velocity,
            force_before,
            trans_send,
            leaving_slots.reshape(1, leaving),
            count_row,
            own,
        ),
        far=4,
        cost=pl.CostEstimate(flops=40 * slots, bytes_accessed=400 * slots, transcendentals=0),
    )
    own, trans_go = run_kernel(
        shock_back_kernel,
        (shaped(3, slots), shaped(2, 3, trans_width)),
        (own, trans, back_first, back_second, shock_spots),
    )
    back = across(trans_go)
    new_force, payload = run_kernel(
        force_kernel,
        (shaped(3, slots), shaped(3, 3, leaving)),
        (half_velocity, displaced, own, back, trans_spots, leaving_spots),
    )
    wide = jax.ShapeDtypeStruct((3, slots), f32)
    disp_next, vel_next, force_next, energy = run_kernel(
        write_kernel,
        (wide, wide, wide, jax.ShapeDtypeStruct((1, slots), f32)),
        (live_count, half_velocity, stay, displaced, new_force, energy),
        far=1,
        cost=pl.CostEstimate(flops=9 * slots, bytes_accessed=80 * slots, transcendentals=0),
    )
    arrivals = along_shock(payload, -1)
    return (disp_next, vel_next, force_next, energy.reshape(slots), arrivals)


def solution(mesh):
    both = ("shock", "trans")
    in_specs = (
        P(None, both),
        P(None, both),
        P(None, both),
        P(),
        P(),
        P(both),
        P(None, both),
        P(None, both),
        P(None, both),
        P(None, both),
        P(both),
        P(both),
    )
    out_specs = (P(None, both), P(None, both), P(None, both), P(both), P(None, None, both))
    return jax.shard_map(shards, mesh=mesh, in_specs=in_specs, out_specs=out_specs, check_vma=False)
```

```python
import math

import jax
import jax.numpy as jnp
from jax import lax
from jax.experimental import pallas as pl
from jax.experimental.pallas import tpu as pltpu
from jax.sharding import PartitionSpec as P


kick_factor = 0.5
drift_step = 0.02
cutoff_radius = 4.2
radial_width = 0.35
radial_centers = (1.4, 1.9, 2.4, 2.9)
moment_scale = 0.25
pair_list = ((0, 0), (0, 1), (0, 2), (0, 3), (1, 1), (1, 2), (1, 3), (2, 2), (2, 3), (3, 3))
degrees = 5
lanes = 128
f32 = jnp.float32
bf16 = jnp.bfloat16


def lattice_list():
    entries = []
    for number in range(8):
        entries.append(
            (1.0 - 2.0 * (number >> 2 & 1), 1.0 - 2.0 * (number >> 1 & 1), 1.0 - 2.0 * (number & 1))
        )
    for axis_pick in range(3):
        for signed in (2.0, -2.0):
            vector = [0.0, 0.0, 0.0]
            vector[axis_pick] = signed
            entries.append(tuple(vector))
    for zero_pick in (2, 1, 0):
        others = [axis_pick for axis_pick in range(3) if axis_pick != zero_pick]
        for leading in (2.0, -2.0):
            for trailing in (2.0, -2.0):
                vector = [0.0, 0.0, 0.0]
                vector[others[0]] = leading
                vector[others[1]] = trailing
                entries.append(tuple(vector))
    return entries


def exponent_list():
    return [
        (p, q, degree - p - q)
        for degree in range(degrees)
        for p in range(degree, -1, -1)
        for q in range(degree - p, -1, -1)
    ]


exponents = exponent_list()


def rows_of(value, count=8):
    return jnp.broadcast_to(value, (count,) + value.shape[1:])


def pick_lanes(table, index):
    return jnp.take_along_axis(table, index, axis=1, mode="promise_in_bounds")


def pick_columns(blocks, column):
    rows = blocks[0].shape[0]
    lane = rows_of(column & (lanes - 1), rows)
    block = rows_of(column >> 7, rows)
    out = jnp.zeros((rows, lanes), f32)
    for number, table in enumerate(blocks):
        out = jnp.where(block == number, pick_lanes(table, lane), out)
    return out


def pad_lanes(value, fill=0):
    rows, width = value.shape
    if width == lanes:
        return value
    return jnp.concatenate([value, jnp.full((rows, lanes - width), fill, value.dtype)], axis=1)


def pad_rows(value, count=8):
    rows = value.shape[0]
    return jnp.concatenate([value, jnp.zeros((count - rows,) + value.shape[1:], value.dtype)], axis=0)


def scatter_product(items, block_count, marks=None):
    sub = lax.broadcasted_iota(jnp.int32, (8, lanes), 0)
    spot = lax.broadcasted_iota(jnp.int32, (lanes, lanes), 0)
    left = []
    right = []
    for value, lane, block in items:
        high = value.astype(bf16).astype(f32)
        part = jnp.where(sub < 3, high, value - high)
        block = rows_of(block)
        left.append(
            jnp.concatenate(
                [jnp.where(block == number, part, 0.0) for number in range(block_count)], axis=0
            ).astype(bf16)
        )
        if marks is not None:
            continue
        right.append(
            jnp.where(spot == jnp.broadcast_to(lane, (lanes, lanes)), 1.0, 0.0).astype(bf16)
        )
    return lax.dot_general(
        jnp.concatenate(left, axis=1),
        jnp.concatenate(right, axis=1) if marks is None else marks,
        (((1,), (1,)), ((), ())),
        preferred_element_type=f32,
    )


def twice(value):
    return jnp.concatenate([value, value, value[:2]], axis=0)


def summed(product, number):
    return product[8 * number : 8 * number + 3] + product[8 * number + 3 : 8 * number + 6]


def start_kernel(disp, vel, force, trans_send, displaced_out, trans_out):
    displaced = disp[...] + drift_step * (vel[...] + kick_factor * force[...])
    displaced_out[...] = displaced
    width = trans_send.shape[1]
    blocks = [
        pad_rows(displaced[:, lanes * b : lanes * (b + 1)]) for b in range(displaced.shape[1] // lanes)
    ]
    for way in range(2):
        column = pad_lanes(trans_send[way : way + 1, :])
        trans_out[way] = pick_columns(blocks, column)[:3, :width]


def prepare_kernel(
    shock_send,
    neighbour_block,
    neighbour_lane,
    beta,
    alpha,
    trans_like,
    shock_spots_out,
    spots_out,
    linear_out,
    matrix_out,
):
    neighbours, slots = neighbour_block.shape
    halves = slots // lanes
    width = trans_like.shape[2]
    column = neighbour_block[...] * lanes + neighbour_lane[...]
    column = jnp.where(column >= slots + 2 * width, column + (lanes - 2 * width), column)
    even = lax.axis_index("shock") % 2 == 0
    border = (halves + 1) * lanes
    turned = column + lanes * (2 * halves + 3) - 2 * (column & -lanes)
    column = jnp.where(even & (column >= border), turned, column)
    column = jnp.where(neighbour_block[...] < 0, -1, column)
    spots_out[...] = jnp.full(spots_out.shape, -1, jnp.int32)
    for number in range(halves):
        spots_out[pl.ds(number, neighbours, stride=halves), :] = column[
            :, lanes * number : lanes * (number + 1)
        ]
    shock_spots_out[0:1, :] = jnp.where(even, shock_send[1:2, :], shock_send[0:1, :])
    shock_spots_out[1:2, :] = jnp.where(even, shock_send[0:1, :], shock_send[1:2, :])
    matrix = alpha[...]
    count = matrix.shape[0]
    matrix = 0.5 * (matrix + matrix.T)
    wide = matrix_out.shape[1] // 3
    matrix = jnp.concatenate([matrix, jnp.zeros((count, wide - count), f32)], axis=1)
    high = matrix.astype(bf16).astype(f32)
    matrix_out[...] = jnp.concatenate([high, high, matrix - high], axis=1).astype(bf16)
    eye = lax.broadcasted_iota(jnp.int32, (count, count), 0) == lax.broadcasted_iota(
        jnp.int32, (count, count), 1
    )
    linear = jnp.sum(
        jnp.where(eye, jnp.broadcast_to(beta[...], (count, count)), 0.0), axis=1, keepdims=True
    )
    linear_out[...] = jnp.broadcast_to(linear, linear_out.shape)


def settle_kernel(
    counts,
    vel,
    force,
    trans_send,
    leaving_slots,
    after,
    half_out,
    kept_out,
    trans_spots_out,
    leaving_out,
):
    slots = vel.shape[1]
    half_out[...] = vel[...] + kick_factor * force[...]
    trans_spots_out[...] = pad_lanes(trans_send[...], -1)
    leaving = leaving_slots.shape[1]
    entry = lax.broadcasted_iota(jnp.int32, (1, leaving), 1)
    going = jnp.where(entry < jnp.broadcast_to(counts[:, 1:2], (1, leaving)), leaving_slots[...], -1)
    leaving_out[...] = pad_lanes(going, -1)
    square = (leaving, leaving)
    eye = lax.broadcasted_iota(jnp.int32, square, 0) == lax.broadcasted_iota(jnp.int32, square, 1)
    upright = jnp.sum(
        jnp.where(eye, jnp.broadcast_to(going, square).astype(f32), 0.0), axis=1, keepdims=True
    )
    slot = lax.broadcasted_iota(jnp.int32, (leaving, slots), 1)
    gone = jnp.where(slot.astype(f32) == jnp.broadcast_to(upright, slot.shape), 1.0, 0.0)
    gone = jnp.sum(gone, axis=0, keepdims=True)
    live = slot[:1] < jnp.broadcast_to(counts[:, 0:1], (1, slots))
    kept_out[...] = jnp.where(live, 1.0 - gone, 0.0)


def mark_kernel(spots, marks_out):
    spot = lax.broadcasted_iota(jnp.int32, (lanes, lanes), 0)
    for row in range(marks_out.shape[1] // lanes):
        lane = jnp.broadcast_to(spots[row : row + 1, :] & (lanes - 1), (lanes, lanes))
        marks_out[:, lanes * row : lanes * (row + 1)] = jnp.where(spot == lane, 1.0, 0.0).astype(bf16)


def shock_kernel(displaced, trans_in, shock_spots, first_out, second_out, trans_block):
    width = trans_in.shape[2]
    trans_block[...] = jnp.zeros(trans_block.shape, f32)
    trans_block[:3, :width] = trans_in[1]
    trans_block[:3, width : 2 * width] = trans_in[0]
    blocks = [
        pad_rows(displaced[:, lanes * b : lanes * (b + 1)]) for b in range(displaced.shape[1] // lanes)
    ]
    blocks.append(trans_block[...])
    for way, out in enumerate((first_out, second_out)):
        out[...] = pick_columns(blocks, shock_spots[way : way + 1, :])[:3]


def energy_kernel(
    displaced,
    trans_in,
    from_first,
    from_second,
    spots,
    linear,
    matrix,
    marks,
    energy_out,
    own_out,
    trans_out,
    first_out,
    second_out,
    trans_block,
    grads,
    packed,
):
    slots = displaced.shape[1]
    width = trans_in.shape[2]
    halves = slots // lanes
    per_group = 8 // halves
    groups = spots.shape[0] // 8
    own_blocks = halves
    block_count = own_blocks + 3
    sub = lax.broadcasted_iota(jnp.int32, (8, lanes), 0)
    half_of = sub % halves
    which = sub // halves

    def by_half(pieces):
        out = rows_of(pieces[0])
        for number in range(1, halves):
            out = jnp.where(half_of == number, rows_of(pieces[number]), out)
        return out

    def by_which(values):
        out = jnp.full((8, lanes), values[0], f32)
        for number in range(1, per_group):
            if any(v != values[0] for v in values):
                out = jnp.where(which == number, values[number], out)
        return out

    def over_group(value):
        shift = 4
        while shift >= halves:
            value = value + pltpu.roll(value, shift, 0)
            shift //= 2
        return value

    trans_block[...] = jnp.zeros(trans_block.shape, f32)
    trans_block[:3, :width] = trans_in[1]
    trans_block[:3, width : 2 * width] = trans_in[0]

    def table(axis):
        pieces = [displaced[axis : axis + 1, lanes * b : lanes * (b + 1)] for b in range(own_blocks)]
        pieces.append(trans_block[axis : axis + 1, :])
        pieces.append(from_first[axis : axis + 1, :])
        pieces.append(from_second[axis : axis + 1, :])
        return pieces

    tables = [table(axis) for axis in range(3)]
    own = [by_half(tables[axis][:own_blocks]) for axis in range(3)]
    spread = [[rows_of(piece) for piece in tables[axis]] for axis in range(3)]
    offsets = lattice_list()
    neighbours = len(offsets)
    offsets = offsets + [offsets[0]] * (groups * per_group - neighbours)

    directions = []
    radials = []
    slopes = []
    inverses = []
    for group in range(groups):
        spot = spots[8 * group : 8 * group + 8, :]
        live = spot >= 0
        lane = jnp.where(live, spot & (lanes - 1), 0)
        block = jnp.where(live, spot >> 7, 0)
        vector = []
        for axis in range(3):
            picked = pick_lanes(spread[axis][0], lane)
            for number in range(1, block_count):
                picked = jnp.where(block == number, pick_lanes(spread[axis][number], lane), picked)
            offset = by_which([offsets[per_group * group + i][axis] for i in range(per_group)])
            vector.append(offset + picked - own[axis])
        square = vector[0] * vector[0] + vector[1] * vector[1] + vector[2] * vector[2]
        inverse = lax.rsqrt(square)
        distance = square * inverse
        directions.append([v * inverse for v in vector])
        inverses.append(inverse)
        angle = distance * (math.pi / cutoff_radius) - (math.pi / 2)
        squared = angle * angle
        sine = jnp.full_like(angle, -1.0 / math.factorial(15))
        for order in (13, 11, 9, 7, 5, 3, 1):
            sine = sine * squared + ((-1.0) ** ((order - 1) // 2)) / math.factorial(order)
        sine = sine * angle
        cosine = jnp.full_like(angle, 1.0 / math.factorial(16))
        for order in (14, 12, 10, 8, 6, 4, 2, 0):
            cosine = cosine * squared + ((-1.0) ** (order // 2)) / math.factorial(order)
        half = jnp.where(live, 0.5, 0.0)
        smooth = half - half * sine
        smooth_slope = half * cosine * (-math.pi / cutoff_radius)
        radial = []
        slope = []
        for center in radial_centers:
            away = (distance - center) * (1.0 / radial_width)
            bell = jnp.exp(-away * away)
            radial.append(smooth * bell)
            slope.append(bell * (smooth_slope - smooth * away * (2.0 / radial_width)))
        radials.append(radial)
        slopes.append(slope)

    scaled = [
        [
            [direction[axis] * (1.0 / power) if power > 1 else direction[axis] for power in range(1, degrees)]
            for axis in range(3)
        ]
        for direction in directions
    ]
    monomials = {}
    kinds = len(radial_centers)
    moments = {}
    for triple in exponents:
        p, q, w = triple
        if p + q + w == 0:
            monomials[triple] = None
        else:
            axis = 0 if p else (1 if q else 2)
            lower = tuple(v - (1 if a == axis else 0) for a, v in enumerate(triple))
            values = []
            for group in range(groups):
                factor = scaled[group][axis][triple[axis] - 1]
                before = monomials[lower]
                values.append(factor if before is None else before[group] * factor)
            monomials[triple] = values
        for kind in range(kinds):
            total = None
            for group in range(groups):
                term = radials[group][kind]
                if monomials[triple] is not None:
                    term = term * monomials[triple][group]
                total = term if total is None else total + term
            moments[kind, triple] = over_group(total)

    weighted = {}
    for triple in exponents:
        weight = moment_scale**2 * math.factorial(sum(triple))
        for power in triple:
            weight *= math.factorial(power)
        for kind in range(kinds):
            weighted[kind, triple] = moments[kind, triple] * weight
    descriptor = []
    for first, second in pair_list:
        for degree in range(degrees):
            total = None
            for triple in exponents:
                if sum(triple) == degree:
                    term = weighted[first, triple] * moments[second, triple]
                    total = term if total is None else total + term
            descriptor.append(total)
    count = len(descriptor)
    padded = packed.shape[1] // 8 * per_group
    for start in range(0, padded, per_group):
        out = descriptor[min(start, count - 1)]
        for number in range(1, per_group):
            out = jnp.where(which == number, descriptor[min(start + number, count - 1)], out)
        packed[0, start * halves : start * halves + 8, :] = out
    features = jnp.concatenate(
        [packed[0, pl.ds(number, count, stride=halves), :] for number in range(halves)], axis=1
    )
    high = features.astype(bf16).astype(f32)
    stacked = jnp.concatenate([pad_rows(part, matrix.shape[1] // 3) for part in (high, features - high, high)], axis=0)
    slope = linear[...] + lax.dot_general(
        matrix[...], stacked.astype(bf16), (((1,), (0,)), ((), ())), preferred_element_type=f32
    )
    energy_out[...] = 0.5 * jnp.sum(features * (linear[...] + slope), axis=0, keepdims=True)
    for number in range(halves):
        packed[1, pl.ds(number, count, stride=halves), :] = slope[:, lanes * number : lanes * (number + 1)]

    sensitivities = []
    for number in range(count):
        sensitivities.append(
            by_half([packed[1, number * halves + h : number * halves + h + 1, :] for h in range(halves)])
        )
    backs = {}
    for triple in exponents:
        degree = sum(triple)
        for kind in range(kinds):
            total = None
            for place, (first, second) in enumerate(pair_list):
                if kind not in (first, second):
                    continue
                other = second if kind == first else first
                term = sensitivities[place * degrees + degree]
                if first == second:
                    term = term + term
                term = term * weighted[other, triple]
                total = term if total is None else total + term
            backs[kind, triple] = total

    sums = [None] * 3
    for group in range(groups):
        along = None
        tangent = [None] * 3
        for triple in exponents:
            mono = None if sum(triple) == 0 else monomials[triple][group]
            weight = None
            rise = None
            for kind in range(kinds):
                back = backs[kind, triple]
                term = slopes[group][kind] * back
                rise = term if rise is None else rise + term
                if mono is not None:
                    term = radials[group][kind] * back
                    weight = term if weight is None else weight + term
            if mono is not None:
                rise = rise * mono
            along = rise if along is None else along + rise
            if mono is None:
                continue
            for axis in range(3):
                if triple[axis] == 0:
                    continue
                lower = tuple(v - (1 if a == axis else 0) for a, v in enumerate(triple))
                term = weight if monomials[lower] is None else weight * monomials[lower][group]
                tangent[axis] = term if tangent[axis] is None else tangent[axis] + term
        direction = directions[group]
        radial_part = (
            direction[0] * tangent[0] + direction[1] * tangent[1] + direction[2] * tangent[2]
        )
        straight = along - radial_part * inverses[group]
        for axis in range(3):
            gradient = direction[axis] * straight + tangent[axis] * inverses[group]
            grads[axis, 8 * group : 8 * group + 8, :] = gradient
            sums[axis] = gradient if sums[axis] is None else sums[axis] + gradient

    items = []
    for row in range(neighbours * halves):
        value = jnp.where(
            (sub == 0) | (sub == 3),
            rows_of(grads[0, row : row + 1, :]),
            jnp.where(
                (sub == 1) | (sub == 4),
                rows_of(grads[1, row : row + 1, :]),
                rows_of(grads[2, row : row + 1, :]),
            ),
        )
        spot = spots[row : row + 1, :]
        items.append((value, spot & (lanes - 1), spot >> 7))
    product = scatter_product(items, block_count, marks[...])
    totals = [over_group(value) for value in sums]
    for number in range(own_blocks):
        self_part = jnp.concatenate([totals[axis][number : number + 1] for axis in range(3)], axis=0)
        own_out[:, lanes * number : lanes * (number + 1)] = summed(product, number) - self_part
    trans_out[...] = summed(product, own_blocks)
    first_out[...] = summed(product, own_blocks + 1)
    second_out[...] = summed(product, own_blocks + 2)


def shock_back_kernel(own, trans, back_first, back_second, shock_spots, own_out, trans_out):
    own_blocks = own.shape[1] // lanes
    width = trans_out.shape[2]
    items = []
    for way, back in enumerate((back_first, back_second)):
        spot = shock_spots[way : way + 1, :]
        items.append((twice(back[...]), spot & (lanes - 1), spot >> 7))
    product = scatter_product(items, own_blocks + 1)
    for number in range(own_blocks):
        cut = slice(lanes * number, lanes * (number + 1))
        own_out[:, cut] = own[:, cut] + summed(product, number)
    ghosts = trans[...] + summed(product, own_blocks)
    trans_out[0] = ghosts[:, :width]
    trans_out[1] = ghosts[:, width : 2 * width]


def force_kernel(half_velocity, displaced, own, back, trans_spots, leaving_spots, force_out, payload_out):
    own_blocks = own.shape[1] // lanes
    items = []
    for way in range(2):
        spot = trans_spots[way : way + 1, :]
        items.append((twice(pad_lanes(back[1 - way])), spot & (lanes - 1), spot >> 7))
    product = scatter_product(items, own_blocks)
    leaving = payload_out.shape[2]
    blocks = []
    for number in range(own_blocks):
        cut = slice(lanes * number, lanes * (number + 1))
        new_force = -(own[:, cut] + summed(product, number))
        force_out[:, cut] = new_force
        new_velocity = half_velocity[:, cut] + kick_factor * new_force
        blocks.append(
            jnp.concatenate(
                [pad_rows(displaced[:, cut]), pad_rows(new_velocity), pad_rows(new_force)], axis=0
            )
        )
    picked = pick_columns(blocks, leaving_spots[...])
    for number in range(3):
        payload_out[number] = picked[8 * number : 8 * number + 3, :leaving]


def write_kernel(half_velocity, kept, displaced, new_force, energy, disp_out, vel_out, force_out, energy_out):
    keep = kept[...]
    force = new_force[...]
    disp_out[...] = displaced[...] * keep
    vel_out[...] = (half_velocity[...] + kick_factor * force) * keep
    force_out[...] = force * keep
    energy_out[...] = energy[...] * keep


def along_shock(x, by):
    devices = lax.axis_size("shock")
    return lax.ppermute(
        x, "shock", [(i, i + by) for i in range(devices) if 0 <= i + by < devices]
    )


def with_partner(x, start):
    devices = lax.axis_size("shock")
    lows = range(start, devices - 1, 2)
    return lax.ppermute(x, "shock", [(i, i + 1) for i in lows] + [(i + 1, i) for i in lows])


def across(x):
    devices = lax.axis_size("trans")
    down = [(i, (i - 1) % devices) for i in range(devices)]
    up = [(i, (i + 1) % devices) for i in range(devices)]
    if sorted(down) == sorted(up):
        return lax.ppermute(x, "trans", down)
    return jnp.stack([lax.ppermute(x[0], "trans", down), lax.ppermute(x[1], "trans", up)])


def shaped(*dims, kind=f32):
    return pltpu.VMEM(dims, kind)


def run_kernel(kernel, out_shape, args, scratch=(), far=0, cost=None):
    vmem = pl.BlockSpec(memory_space=pltpu.VMEM)
    args = [
        arg if place < far else pltpu.with_memory_space_constraint(arg, pltpu.VMEM)
        for place, arg in enumerate(args)
    ]
    return pl.pallas_call(
        kernel,
        in_specs=[vmem] * len(args),
        out_specs=tuple(vmem for _ in out_shape),
        out_shape=out_shape,
        scratch_shapes=list(scratch),
        cost_estimate=cost,
    )(*args)


def shards(
    displacement,
    velocity,
    force_before,
    beta,
    alpha,
    live_count,
    trans_send,
    shock_send,
    neighbour_block,
    neighbour_lane,
    leaving_slots,
    leaving_count,
):
    slots = displacement.shape[1]
    trans_width = trans_send.shape[1]
    shock_width = shock_send.shape[1]
    neighbours = neighbour_block.shape[0]
    leaving = leaving_slots.shape[0]
    halves = slots // lanes
    groups = -(-neighbours // (8 // halves))
    count = len(pair_list) * degrees
    assert slots % lanes == 0 and 8 % halves == 0 and halves <= 4
    assert shock_width == lanes and 2 * trans_width <= lanes
    displaced, trans_go = run_kernel(
        start_kernel,
        (shaped(3, slots), shaped(2, 3, trans_width)),
        (displacement, velocity, force_before, trans_send),
        far=4,
    )
    trans_in = across(trans_go)
    whole = jnp.int32
    shock_spots, spots, linear, matrix = run_kernel(
        prepare_kernel,
        (
            shaped(2, shock_width, kind=whole),
            shaped(groups * 8, lanes, kind=whole),
            shaped(count, slots),
            shaped(count, 3 * (-(-count // 8) * 8), kind=bf16),
        ),
        (shock_send, neighbour_block, neighbour_lane, beta.reshape(1, count), alpha, trans_go),
        far=5,
        cost=pl.CostEstimate(flops=40 * slots * neighbours, bytes_accessed=12 * slots * neighbours, transcendentals=0),
    )
    to_first, to_second = run_kernel(
        shock_kernel,
        (shaped(3, shock_width), shaped(3, shock_width)),
        (displaced, trans_in, shock_spots),
        (pltpu.VMEM((8, lanes), f32),),
    )
    from_second = with_partner(to_second, 1)
    from_first = with_partner(to_first, 0)
    (marks,) = run_kernel(
        mark_kernel,
        (shaped(lanes, neighbours * slots, kind=bf16),),
        (spots,),
        cost=pl.CostEstimate(
            flops=2 * lanes * neighbours * slots, bytes_accessed=2 * lanes * neighbours * slots, transcendentals=0
        ),
    )
    packed_rows = -(-(count * halves) // 8) * 8
    energy, own, trans, first, second = run_kernel(
        energy_kernel,
        (shaped(1, slots), shaped(3, slots), shaped(3, lanes), shaped(3, lanes), shaped(3, lanes)),
        (displaced, trans_in, from_first, from_second, spots, linear, matrix, marks),
        (
            pltpu.VMEM((8, lanes), f32),
            pltpu.VMEM((3, groups * 8, lanes), f32),
            pltpu.VMEM((2, packed_rows, lanes), f32),
        ),
    )
    back_second = with_partner(second, 1)
    back_first = with_partner(first, 0)
    half_velocity, kept, trans_spots, leaving_spots = run_kernel(
        settle_kernel,
        (
            shaped(3, slots),
            shaped(1, slots),
            shaped(2, lanes, kind=whole),
            shaped(1, lanes, kind=whole),
        ),
        (
            jnp.concatenate([live_count, leaving_count]).reshape(1, 2),
            velocity,
            force_before,
            trans_send,
            leaving_slots.reshape(1, leaving),
            own,
        ),
        far=5,
        cost=pl.CostEstimate(flops=40 * slots, bytes_accessed=400 * slots, transcendentals=0),
    )
    own, trans_go = run_kernel(
        shock_back_kernel,
        (shaped(3, slots), shaped(2, 3, trans_width)),
        (own, trans, back_first, back_second, shock_spots),
    )
    back = across(trans_go)
    new_force, payload = run_kernel(
        force_kernel,
        (shaped(3, slots), shaped(3, 3, leaving)),
        (half_velocity, displaced, own, back, trans_spots, leaving_spots),
    )
    wide = jax.ShapeDtypeStruct((3, slots), f32)
    disp_next, vel_next, force_next, energy = run_kernel(
        write_kernel,
        (wide, wide, wide, jax.ShapeDtypeStruct((1, slots), f32)),
        (half_velocity, kept, displaced, new_force, energy),
        cost=pl.CostEstimate(flops=9 * slots, bytes_accessed=80 * slots, transcendentals=0),
    )
    arrivals = along_shock(payload, -1)
    return (disp_next, vel_next, force_next, energy.reshape(slots), arrivals)


def solution(mesh):
    both = ("shock", "trans")
    in_specs = (
        P(None, both),
        P(None, both),
        P(None, both),
        P(),
        P(),
        P(both),
        P(None, both),
        P(None, both),
        P(None, both),
        P(None, both),
        P(both),
        P(both),
    )
    out_specs = (P(None, both), P(None, both), P(None, both), P(both), P(None, None, both))
    return jax.shard_map(shards, mesh=mesh, in_specs=in_specs, out_specs=out_specs, check_vma=False)
```
